32 devices in a mesh: groups: 2 (over y), brick: 4 (over z), chan: 2 (over x), sub: 2 (over core).
Axes of the slice: x: 2, y: 2, z: 4, core: 2. Of those that a mesh axis runs over, the one named last changes fastest.
Arguments:
- features: bfloat16 [16384, 256], P(('groups', 'brick', 'chan', 'sub')), parts along dimension 0, may hold values from -6 to 6
- scan_order: int32 [32, 512], P(('groups', 'brick', 'chan', 'sub')), parts along dimension 0, may hold values from 0 to 511, each once within a row
- kernel_map: int32 [256, 27], P(('groups', 'brick', 'sub')), parts along dimension 0, may hold values from 0 to 20, as said below
- halo_send: int32 [32, 2], P(('groups', 'brick', 'sub')), parts along dimension 0, may hold values from 0 to 15, as said below
- down_route: int32 [256, 1], P(('groups', 'brick', 'sub')), parts along dimension 0, may hold values from 0 to 7; in each aligned block of 16 rows (0 to 15, 16 to 31, ...) at most 4 rows name the same one
- conv1_weight: bfloat16 [27, 256, 256], P(None, 'chan'), may hold values from -0.078125 to 0.078125
- conv2_weight: bfloat16 [27, 256, 256], P(None, 'chan'), may hold values from -0.078125 to 0.078125
- down_weight: bfloat16 [8, 256, 256], P(None, 'chan'), may hold values from -0.125 to 0.125
- gain_first: float32 [256], P('chan'), may hold values from 0.1 to 1.9
- bias_first: float32 [256], P('chan'), may hold values from -3 to 3
- gain_second: float32 [256], P('chan'), may hold values from 0.1 to 1.9
- bias_second: float32 [256], P('chan'), may hold values from -3 to 3
- gain_down: float32 [256], P('chan'), may hold values from 0.1 to 1.9
- bias_down: float32 [256], P('chan'), may hold values from -3 to 3
Outputs:
- coarse_out: bfloat16 [16, 256, 256], P(('groups', 'brick', 'sub'), 'chan'), parts along dimension 0
The draws below stay inside these ranges and needn't reach their ends.
There are 2 independent parts, one for each index of `groups`. The reference program is written for one: setup_inputs(seed, part) draws one part's arguments, and reference() takes and returns one part's arrays. A program takes and returns all parts, laid end to end along the dimension named above; an argument that names none is the same for every part. Nothing has to cross between parts.
Inputs may be any that keep to these rules, and one draw needn't show every extreme that they name: `scan_order`: each row is an order of the 512 local rows of one device, each once. `kernel_map`: entries index an owner's extended list: own blocks below 16, then 2 blocks from the previous owner, 2 from the next, and 20 for an absent neighbour block. Offset 13 of block n always names n itself. `halo_send`: row 2 o lists the blocks owner o sends to owner o + 1, row 2 o + 1 those it sends to owner o - 1; each row names 2 distinct blocks. `down_route`: within the 16 rows of one owner no destination is named by more than 4 rows.
All inputs are finite; a program needn't handle non-finite values.
Results may differ from the reference program's by a relative error of at most 0.014.
Values may be sent and summed in bfloat16 or wider, within the bound.
A program may use at most 64 MiB of HBM per device.

```python
import math
import jax
import jax.numpy as jnp
import numpy as np
from jax import lax

C = 256
K = 27
BLK = 64
SCAN_DEV = 512
OWNERS = 8
SCAN_DEVS = 16
SCAN_ROWS = 8192
NB_OWN = 16
HCAP = 2
NB_EXT = 20
DCAP = 4
N_BRICK = 4
N_CHAN = 2
N_SUB = 2


def draw_kernel_map(key, part):
    key_kind, key_own, key_rim = jax.random.split(key, 3)
    shape = (OWNERS, NB_OWN, K)
    choose = jax.random.randint(key_kind, shape, 0, 10)
    own_block = jax.random.randint(key_own, shape, 0, NB_OWN)
    rim_block = jax.random.randint(key_rim, shape, NB_OWN, NB_EXT)
    table = jnp.where(choose < 4, own_block, jnp.where(choose < 6, rim_block, NB_EXT))
    block_index = jnp.arange(NB_OWN, dtype=jnp.int32)[None, :, None]
    offset_index = jnp.arange(K, dtype=jnp.int32)[None, None, :]
    table = jnp.where(offset_index == 13, block_index, table)
    table = jnp.where((offset_index == 0) & (block_index < 2 * HCAP), NB_OWN + block_index, table)
    return table.reshape(OWNERS * NB_OWN, K).astype(jnp.int32)


def pick_blocks(subkey):
    return jax.random.permutation(subkey, NB_OWN)


def draw_halo_send(key, part):
    subkeys = jax.random.split(key, OWNERS * 2)
    orders = jax.vmap(pick_blocks)(subkeys)
    return orders[:, :HCAP].astype(jnp.int32)


def levels(stream_key, extent, cuts, least, largest):
    factor_of = 1.0
    for dim, blocks in cuts:
        steps = jax.random.uniform(jax.random.fold_in(jax.random.fold_in(stream_key, 6), dim), (blocks,), jnp.float32, least / len(cuts), largest / len(cuts))
        factor_of = factor_of * jnp.repeat(jnp.exp(steps), extent[dim] // blocks).reshape((-1,) + (1,) * (len(extent) - 1 - dim))
    return factor_of


def shared_out(rng, own, number, rows, amount, top, limit, skew):
    ranking = jax.random.permutation(rng, amount)
    crowded, usual = portions_of(amount, rows * top, limit, skew, True), portions_of(amount, rows * top, limit, skew, False)
    places = jnp.arange(amount)

    def named(lengths, offset_by):
        used = int((lengths > 0).sum())
        fixed = max(1, used // 4)
        passed = fixed + (places - fixed + offset_by * (used - fixed)) % max(1, amount - fixed)
        return jnp.zeros((amount,), jnp.int32).at[ranking[jnp.where(places < fixed, places, passed)]].set(jnp.asarray(lengths, jnp.int32))

    lengths = jnp.where(number % 4 == 0, named(crowded, number // 4), named(usual, number - number // 4 - 1))
    mixed = jax.random.permutation(jax.random.fold_in(own, 3), amount)
    giver, receiver = mixed[0:amount // 2 * 2:2], mixed[1:amount // 2 * 2:2]
    slack = jnp.minimum(lengths[giver] - 1, limit - lengths[receiver]) // 2
    slack = jnp.where((giver == ranking[0]) | (receiver == ranking[0]) | (lengths[receiver] == 0), 0, jnp.maximum(slack, 0))
    passed = jax.random.randint(jax.random.fold_in(own, 4), (amount // 2,), 0, 1 << 20) % (slack + 1)
    lengths = lengths.at[giver].add(-passed).at[receiver].add(passed)
    items = jnp.searchsorted(jnp.cumsum(lengths), jnp.arange(rows * top), side="right").astype(jnp.int32)
    grid = items.reshape(top, rows).T
    grid = grid[jax.random.permutation(jax.random.fold_in(own, 1), rows)]
    offset_by = jax.random.randint(jax.random.fold_in(own, 2), (rows, 1), 0, top)
    return jnp.take_along_axis(grid, (jnp.arange(top)[None, :] + offset_by) % top, axis=1)


def portions_of(amount, total, limit, slope, full):
    portions = [(1 << 20) // math.isqrt(grade ** slope) + 1 for grade in range(1, amount + 1)]
    largest = limit if full else min(limit, max(-(-total // amount), total * portions[0] // sum(portions)))
    least = 1 if total - largest >= amount - 1 else 0
    holding, rest = [largest] + [least] * (amount - 1), total - largest - least * (amount - 1)
    while rest > 0:
        free = [i for i in range(1, amount) if holding[i] < largest] or [i for i in range(1, amount) if holding[i] < limit]
        pool, left = sum([portions[i] for i in free]), rest
        for i in free:
            extra = min(limit - holding[i], max(1, left * portions[i] // pool), rest)
            holding[i] = holding[i] + extra
            rest = rest - extra
    return np.array(holding)


def centred(rng, shape, deviation, limit, cuts=(), kind=jnp.bfloat16):
    factor_of = levels(rng, shape, cuts, -0.22, 0.18) if cuts else 1.0
    drawn = jax.random.normal(rng, shape, jnp.float32) * deviation * factor_of
    return jnp.minimum(jnp.maximum(drawn, -limit), limit).astype(kind)


def setup_inputs(seed: int = 0, part: int = 0) -> dict:
    keys = jax.random.split(jax.random.key(seed), 15)
    own_keys = jax.random.split(jax.random.fold_in(keys[14], part), 15)
    features = centred(own_keys[0], (SCAN_ROWS, C), 1.0, 6.0, ((0, 16),))
    scan_order = jax.vmap(lambda own: jax.random.permutation(own, SCAN_DEV))(jax.random.split(own_keys[1], SCAN_DEVS)).reshape((SCAN_DEVS, SCAN_DEV)).astype(jnp.int32)
    kernel_map = draw_kernel_map(jax.random.fold_in(jax.random.fold_in(keys[14], part), 71), part)
    halo_send = draw_halo_send(jax.random.fold_in(jax.random.fold_in(keys[14], part), 71), part)
    down_route_keys = jax.random.split(jax.random.fold_in(own_keys[4], 1), (OWNERS * NB_OWN) // NB_OWN)
    down_route_turns = jax.random.permutation(jax.random.fold_in(own_keys[4], 3), (OWNERS * NB_OWN) // NB_OWN)
    down_route = jax.vmap(lambda own, number: shared_out(jax.random.fold_in(own_keys[4], 2), own, number, NB_OWN, OWNERS, 1, DCAP, 2))(down_route_keys, down_route_turns).reshape((OWNERS * NB_OWN, 1))
    conv1_weight = centred(keys[5], (K, C, C), (K * C) ** -0.5, 0.078125, ((1, 2),))
    conv2_weight = centred(keys[6], (K, C, C), (K * C) ** -0.5, 0.078125, ((1, 2),))
    down_weight = centred(keys[7], (8, C, C), (8 * C) ** -0.5, 0.125, ((1, 2),))
    gain_first = jnp.clip(1.0 + 0.18 * jax.random.normal(keys[8], (C,), jnp.float32), 0.1, 1.9)
    bias_first = centred(keys[9], (C,), 0.5, 3.0, ((0, 2),), jnp.float32)
    gain_second = jnp.clip(1.0 + 0.18 * jax.random.normal(keys[10], (C,), jnp.float32), 0.1, 1.9)
    bias_second = centred(keys[11], (C,), 0.5, 3.0, ((0, 2),), jnp.float32)
    gain_down = jnp.clip(1.0 + 0.18 * jax.random.normal(keys[12], (C,), jnp.float32), 0.1, 1.9)
    bias_down = centred(keys[13], (C,), 0.5, 3.0, ((0, 2),), jnp.float32)
    return {"features": features, "scan_order": scan_order, "kernel_map": kernel_map, "halo_send": halo_send, "down_route": down_route, "conv1_weight": conv1_weight, "conv2_weight": conv2_weight, "down_weight": down_weight, "gain_first": gain_first, "bias_first": bias_first, "gain_second": gain_second, "bias_second": bias_second, "gain_down": gain_down, "bias_down": bias_down}


def extend_blocks(blocks, halo_send):
    owners = blocks.shape[0]
    sends = halo_send.reshape(owners, 2, -1)
    upward = jax.vmap(lambda source, chosen: source[chosen])(blocks, sends[:, 0])
    downward = jax.vmap(lambda source, chosen: source[chosen])(blocks, sends[:, 1])
    zeros_rim = jnp.zeros_like(upward[:1])
    from_lower = jnp.concatenate([zeros_rim, upward[:-1]], axis=0)
    from_upper = jnp.concatenate([downward[1:], zeros_rim], axis=0)
    empty_block = jnp.zeros_like(blocks[:, :1])
    return jnp.concatenate([blocks, from_lower, from_upper, empty_block], axis=1)


def convolve(extended, weight, kernel_map):
    owners = extended.shape[0]
    tables = kernel_map.reshape(owners, -1, K)
    weight_wide = weight.astype(jnp.float32)
    offsets = jnp.arange(K, dtype=jnp.int32)[:, None]

    def one_owner(inputs):
        blocks, table = inputs
        product = jnp.einsum("brc,kdc->kbrd", blocks.astype(jnp.float32), weight_wide, precision=lax.Precision.HIGHEST)
        picked = product[offsets, table.T]
        return jnp.sum(picked, axis=0)

    return lax.map(one_owner, (extended, tables))


def reference(features, scan_order, kernel_map, halo_send, down_route, conv1_weight, conv2_weight, down_weight, gain_first, bias_first, gain_second, bias_second, gain_down, bias_down):
    owners = N_BRICK * N_SUB
    per_owner = SCAN_DEV // owners
    scan_grid = features.reshape(N_BRICK, N_CHAN, N_SUB, SCAN_DEV, C)
    orders = scan_order.reshape(N_BRICK, N_CHAN, N_SUB, SCAN_DEV, 1)
    ordered = jnp.take_along_axis(scan_grid, orders, axis=3)
    ordered = ordered.reshape(N_BRICK, N_CHAN, N_SUB, owners, per_owner, C)
    owner_rows = ordered.transpose(3, 0, 2, 1, 4, 5).reshape(owners, NB_OWN, BLK, C)
    conv_first = convolve(extend_blocks(owner_rows, halo_send), conv1_weight, kernel_map)
    hidden = jax.nn.relu(conv_first * gain_first + bias_first).astype(jnp.bfloat16)
    second = convolve(extend_blocks(hidden, halo_send), conv2_weight, kernel_map)
    refined = jax.nn.relu(second * gain_second + bias_second + owner_rows.astype(jnp.float32)).astype(jnp.bfloat16)
    children = refined.reshape(owners, NB_OWN, 8, 8, C).astype(jnp.float32)
    coarse = jnp.einsum("snoqi,oic->scnq", children, down_weight.astype(jnp.float32), precision=lax.Precision.HIGHEST)
    tile_values = jax.nn.relu(coarse * gain_down[:, None, None] + bias_down[:, None, None]).astype(jnp.bfloat16)
    destination = down_route.reshape(owners, NB_OWN)
    onehot = (destination[:, :, None] == jnp.arange(owners, dtype=jnp.int32)[None, None, :]).astype(jnp.int32)
    earlier = jnp.sum((jnp.cumsum(onehot, axis=1) - onehot) * onehot, axis=2)
    position = destination * DCAP + earlier
    selector = (position[:, None, :] == jnp.arange(owners * DCAP, dtype=jnp.int32)[None, :, None]).astype(jnp.float32)
    outgoing = jnp.einsum("spn,scnq->scpq", selector, tile_values.astype(jnp.float32), precision=lax.Precision.HIGHEST)
    outgoing = outgoing.reshape(owners, C, owners, DCAP * 8).transpose(2, 1, 0, 3)
    return outgoing.reshape(owners, C, owners * DCAP * 8).astype(jnp.bfloat16)
```

```python
import functools

import jax
import jax.numpy as jnp
from jax import lax
from jax.experimental import pallas as pl
from jax.experimental.pallas import tpu as pltpu
from jax.sharding import PartitionSpec as P

BLK = 64
LANES = 128
MESH = pl.DeviceIdType.MESH


def products(lhs, weight, prod, place):
    width = prod.shape[3]
    shape = (lhs.shape[0] // BLK, BLK, width)

    def step(pair, carry):
        both = weight[pl.ds(pl.multiple_of(pair * 2 * width, 2 * width), 2 * width), :]
        result = lax.dot_general(
            lhs, both, (((1,), (1,)), ((), ())), preferred_element_type=jnp.float32
        )
        prod[2 * pair, place] = result[:, :width].reshape(shape)
        prod[2 * pair + 1, place] = result[:, width:].reshape(shape)
        return carry

    lax.fori_loop(0, prod.shape[0] // 2, step, 0, unroll=True)


def gathered_sum(prod, kernel_map, n):
    total = None
    for k in range(kernel_map.shape[1]):
        term = prod[k, kernel_map[n, k]]
        total = term if total is None else total + term
    return total


def flip(x, bits):
    result = x
    weight = 1
    while weight <= bits:
        if bits & weight:
            result = result + weight - 2 * weight * lax.rem(lax.div(x, weight), 2)
        weight *= 2
    return result


def fused_kernel(
    axes,
    features_hbm,
    scan_order_hbm,
    kernel_map_hbm,
    halo_send_hbm,
    down_route_hbm,
    conv1_hbm,
    conv2_hbm,
    down_hbm,
    gain_first_hbm,
    bias_first_hbm,
    gain_second_hbm,
    bias_second_hbm,
    gain_down_hbm,
    bias_down_hbm,
    out,
    features,
    scan_order,
    kernel_map,
    halo_send,
    down_route,
    gain_first,
    bias_first,
    gain_second,
    bias_second,
    gain_down,
    bias_down,
    stage_sem,
    conv1_w,
    conv2_w,
    down_w,
    ordered,
    ext,
    halo_out,
    halo_in,
    hid_own,
    hid_in,
    hid_halo_out,
    hid_halo_in,
    prod,
    kids_ref,
    part,
    selector,
    tile_out,
    tile_in,
    w_sem,
    a2a_s,
    a2a_r,
    fwd_s,
    fwd_r,
    halo_s,
    halo_r,
    hid_s,
    hid_r,
    hh_s,
    hh_r,
    tile_s,
    tile_r,
):
    staged = [
        pltpu.make_async_copy(source, place, stage_sem.at[i])
        for i, (source, place) in enumerate(
            [
                (features_hbm, features),
                (scan_order_hbm, scan_order),
                (kernel_map_hbm, kernel_map),
                (halo_send_hbm, halo_send),
                (down_route_hbm, down_route),
                (gain_first_hbm, gain_first),
                (bias_first_hbm, bias_first),
                (gain_second_hbm, gain_second),
                (bias_second_hbm, bias_second),
                (gain_down_hbm, gain_down),
                (bias_down_hbm, bias_down),
            ]
        )
    ]
    for load in staged:
        load.start()
    n_brick, n_chan, n_sub = axes
    owners = n_brick * n_sub
    blocks = kernel_map.shape[0]
    channels = features.shape[1]
    width = out.shape[1]
    hcap = halo_send.shape[1]
    group_count = hid_s.shape[1]
    group = blocks // group_count
    me_group = lax.axis_index("groups")
    chan = lax.axis_index("chan")
    me = lax.axis_index("brick") * n_sub + lax.axis_index("sub")
    own_cols = pl.ds(pl.multiple_of(chan * width, LANES), width)

    def device(owner, c):
        return (me_group, lax.div(owner, n_sub), c, lax.rem(owner, n_sub))

    def owner_at(shift):
        return lax.rem(me + shift + owners, owners)

    def chan_at(shift):
        return lax.rem(chan + shift + n_chan, n_chan)

    def remote(src, dst, send, recv, target):
        return pltpu.make_async_remote_copy(
            src_ref=src,
            dst_ref=dst,
            send_sem=send,
            recv_sem=recv,
            device_id=target,
            device_id_type=MESH,
        )

    taps = kernel_map.shape[1]
    loads = [
        pltpu.make_async_copy(conv1_hbm, conv1_w.at[pl.ds(0, taps * width)], w_sem.at[0]),
        pltpu.make_async_copy(down_hbm, down_w, w_sem.at[1]),
    ]

    def cols_from(j):
        return pl.ds(pl.multiple_of(chan_at(-j) * width, LANES), width)

    for j in range(n_chan):
        target = conv2_w.at[pl.ds(0, taps * width), pl.ds(j * width, width)]
        loads.append(
            pltpu.make_async_copy(conv2_hbm.at[:, cols_from(j)], target, w_sem.at[2 + j])
        )
    barrier = pltpu.get_barrier_semaphore()
    partners = [device(flip(me, i), chan) for i in range(1, owners)]
    partners += [device(me, chan_at(j)) for j in range(1, n_chan)]
    partners += [device(owner_at(d), chan_at(j)) for j in range(1, n_chan) for d in (1, -1)]
    for partner in partners:
        pl.semaphore_signal(barrier, inc=1, device_id=partner, device_id_type=MESH)
    for load in loads:
        load.start()

    for load in staged[:2]:
        load.wait()
    count = features.shape[0]
    source_row = lax.broadcasted_iota(jnp.int32, (count, count), 0)
    chosen = jnp.where(source_row == scan_order[...], 1.0, 0.0).astype(jnp.bfloat16)
    rows = lax.dot_general(
        chosen, features[...], (((0,), (0,)), ((), ())), preferred_element_type=jnp.float32
    ).astype(jnp.bfloat16)
    ordered[...] = rows.reshape(owners, BLK, channels)

    pl.semaphore_wait(barrier, len(partners))

    pending = []
    a2a = []
    for i in range(1, owners):
        target = flip(me, i)
        a2a.append(
            remote(
                ordered.at[target],
                ext.at[me * n_chan + chan],
                a2a_s.at[i - 1],
                a2a_r.at[i - 1],
                device(target, chan),
            )
        )
    for copy in a2a:
        copy.start()
    pending += a2a

    def forward(i, src):
        block = flip(me, i) * n_chan + chan
        for j in range(1, n_chan):
            copy = remote(
                src,
                ext.at[block],
                fwd_s.at[j - 1, i],
                fwd_r.at[j - 1, i],
                device(me, chan_at(j)),
            )
            copy.start()
            forwards[i].append(copy)

    forwards = [[] for _ in range(owners)]
    brick_blocks = n_sub * n_chan

    def pass_on(m):
        for i in range(m * n_sub, (m + 1) * n_sub):
            if i == 0:
                forward(0, ordered.at[me])
                ext[me * n_chan + chan] = ordered[me]
            else:
                a2a[i - 1].wait_recv()
                forward(i, ext.at[flip(me, i) * n_chan + chan])

    def collect(m):
        for i in range(m * n_sub, (m + 1) * n_sub):
            for copy in forwards[i]:
                copy.wait_recv()

    def multiply(m):
        place = pl.ds(flip(lax.axis_index("brick"), m) * brick_blocks, brick_blocks)
        products(ext[place].reshape(brick_blocks * BLK, channels), conv1_w, prod, place)

    pass_on(0)
    spare = conv1_w.shape[0] - taps * width
    if spare:
        conv1_w[pl.ds(taps * width, spare), :] = jnp.zeros((spare, channels), jnp.bfloat16)
        conv2_w[pl.ds(taps * width, spare), :] = jnp.zeros((spare, channels), jnp.bfloat16)
    for k in range(taps):
        prod[k, blocks + 2 * hcap] = jnp.zeros((BLK, width), jnp.float32)

    for load in staged[2:]:
        load.wait()
    slots = tile_out.shape[2]
    kids = down_w.shape[0]
    cells = BLK // kids
    capacity = slots // cells
    column = lax.broadcasted_iota(jnp.int32, (1, blocks * cells), 1)
    target_row = lax.rem(column, cells)
    names = [down_route[0, n] for n in range(blocks)]
    for n in range(blocks):
        earlier = jnp.int32(0)
        for before in range(n):
            earlier = earlier + jnp.where(names[before] == names[n], 1, 0)
        position = (names[n] * capacity + earlier) * cells
        target_row = target_row + jnp.where(lax.div(column, cells) == n, position, 0)
    slot_row = lax.broadcasted_iota(jnp.int32, (owners * slots, blocks * cells), 0)
    selector[...] = jnp.where(slot_row == target_row, 1.0, 0.0).astype(jnp.bfloat16)
    loads[0].wait()
    for m in range(1, n_brick):
        pass_on(m)
        collect(m - 1)
        multiply(m - 1)
    collect(n_brick - 1)
    pending += [copy for copies in forwards for copy in copies]

    has_next, has_last = me < owners - 1, me > 0

    def halo_copies(direction):
        return remote(
            halo_out.at[direction],
            halo_in.at[direction],
            halo_s.at[direction],
            halo_r.at[direction],
            device(owner_at(1 if direction == 0 else -1), chan),
        )

    for direction, sends in ((0, has_next), (1, has_last)):
        for j in range(hcap):
            halo_out[direction, j] = ext[halo_send[direction, j]]
        pl.when(sends)(lambda direction=direction: halo_copies(direction).start())
    multiply(n_brick - 1)
    for direction, receives in ((0, has_last), (1, has_next)):

        @pl.when(receives)
        def _():
            halo_copies(direction).wait_recv()

        @pl.when(jnp.logical_not(receives))
        def _():
            halo_in[direction] = jnp.zeros((hcap, BLK, channels), jnp.bfloat16)

    rim = pl.ds(blocks, 2 * hcap)
    products(halo_in[...].reshape(2 * hcap * BLK, channels), conv1_w, prod, rim)

    def first_hidden(n):
        scaled = gathered_sum(prod, kernel_map, n) * gain_first[...] + bias_first[...]
        return jnp.maximum(scaled, 0.0).astype(jnp.bfloat16)

    def hid_halo_copies(direction):
        return [
            remote(
                hid_halo_out.at[direction],
                hid_halo_in.at[direction, j],
                hh_s.at[direction, j],
                hh_r.at[direction, j],
                device(owner_at(1 if direction == 0 else -1), chan_at(j)),
            )
            for j in range(n_chan)
        ]

    for direction, sends in ((0, has_next), (1, has_last)):
        for j in range(hcap):
            hid_halo_out[direction, j] = first_hidden(halo_send[direction, j])

        @pl.when(sends)
        def _():
            for copy in hid_halo_copies(direction):
                copy.start()

    hid_copies = []
    for g in range(group_count):

        def first_block(n, carry):
            hid_own[n] = first_hidden(n)
            return carry

        lax.fori_loop(g * group, (g + 1) * group, first_block, 0)
        place = pl.ds(g * group, group)
        for j in range(1, n_chan):
            copy = remote(
                hid_own.at[place],
                hid_in.at[j - 1, place],
                hid_s.at[j - 1, g],
                hid_r.at[j - 1, g],
                device(me, chan_at(j)),
            )
            copy.start()
            hid_copies.append(copy)
    pending += hid_copies

    for load in loads[2:]:
        load.wait()
    def second_products(g):
        place = pl.ds(g * group, group)
        halves = [hid_own[place]]
        for j in range(1, n_chan):
            hid_copies[g * (n_chan - 1) + j - 1].wait_recv()
            halves.append(hid_in[j - 1, place])
        lhs = jnp.concatenate([half.reshape(group * BLK, width) for half in halves], axis=1)
        products(lhs, conv2_w, prod, place)

    for g in range(group_count - 1):
        second_products(g)
    for direction, receives in ((0, has_last), (1, has_next)):

        @pl.when(receives)
        def _():
            for copy in hid_halo_copies(direction):
                copy.wait_recv()

        @pl.when(jnp.logical_not(receives))
        def _():
            hid_halo_in[direction] = jnp.zeros(hid_halo_in.shape[1:], jnp.bfloat16)

    halves = [hid_halo_in[:, j].reshape(2 * hcap * BLK, width) for j in range(n_chan)]
    products(jnp.concatenate(halves, axis=1), conv2_w, prod, rim)
    second_products(group_count - 1)
    loads[1].wait()

    def second_block(n, carry):
        second = gathered_sum(prod, kernel_map, n)
        residual = ext[n, :, own_cols].astype(jnp.float32)
        refined = jnp.maximum(second * gain_second[...] + bias_second[...] + residual, 0.0)
        refined = refined.reshape(kids, cells, width)
        for o in range(kids):
            kids_ref[o, n] = refined[o]
        return carry

    lax.fori_loop(0, blocks, second_block, 0)
    partial = None
    for o in range(kids):
        child = kids_ref[o].reshape(blocks * cells, width).astype(jnp.bfloat16)
        product = jnp.dot(child, down_w[o], preferred_element_type=jnp.float32)
        partial = product if partial is None else partial + product
    part[...] = partial
    scaled = part[:, own_cols] * gain_down[...] + bias_down[...]
    sides = [scaled.astype(jnp.bfloat16)]
    for j in range(1, n_chan):
        cols = pl.ds(pl.multiple_of(chan_at(j) * width, LANES), width)
        sides.append(part[:, cols].astype(jnp.bfloat16))
    outgoing = jnp.dot(
        selector[...], jnp.concatenate(sides, axis=1), preferred_element_type=jnp.float32
    ).astype(jnp.bfloat16)
    for j in range(n_chan):
        tile_out[j] = outgoing[:, j * width : (j + 1) * width].reshape(owners, slots, width)
    tile_copies = []
    for i in reversed(range(owners)):
        target = flip(me, i)
        for j in range(n_chan):
            if i or j:
                copy = remote(
                    tile_out.at[j, target],
                    tile_in.at[j, me],
                    tile_s.at[j, i],
                    tile_r.at[j, i],
                    device(target, chan_at(j)),
                )
                copy.start()
                tile_copies.append(copy)
    tile_in[0, me] = tile_out[0, me]
    for copy in pending:
        copy.wait_send()
    for direction, sends in ((0, has_next), (1, has_last)):

        @pl.when(sends)
        def _():
            halo_copies(direction).wait_send()
            for copy in hid_halo_copies(direction):
                copy.wait_send()

    for copy in tile_copies:
        copy.wait_recv()
    arrived = tile_in[0].reshape(owners * slots, width).astype(jnp.float32)
    for j in range(1, n_chan):
        other = tile_in[j].reshape(owners * slots, width).astype(jnp.float32)
        arrived = arrived + other * gain_down[...]
    out[0] = jnp.maximum(arrived, 0.0).T.astype(jnp.bfloat16)
    for copy in tile_copies:
        copy.wait_send()


def fused(axes, features, scan_order, kernel_map, halo_send, down_route, w1, w2, wd, *scales):
    n_brick, n_chan, n_sub = axes
    owners = n_brick * n_sub
    blocks = kernel_map.shape[0]
    channels = features.shape[1]
    width = w1.shape[1]
    hcap = halo_send.shape[1]
    taps = kernel_map.shape[1]
    even_taps = taps + taps % 2
    cells = BLK // wd.shape[0]
    slots = max(2, 2 * blocks // owners) * cells
    groups = 4
    bf16, f32 = jnp.bfloat16, jnp.float32
    vmem = pl.BlockSpec(memory_space=pltpu.VMEM)
    hbm = pl.BlockSpec(memory_space=pl.ANY)

    def pair(*shape):
        return [pltpu.SemaphoreType.DMA(shape), pltpu.SemaphoreType.DMA(shape)]

    return pl.pallas_call(
        functools.partial(fused_kernel, axes),
        out_shape=pltpu.VMEM((1, width, owners * slots), bf16),
        in_specs=[hbm] * 14,
        out_specs=vmem,
        scratch_shapes=[
            pltpu.VMEM(features.shape, bf16),
            pltpu.VMEM(scan_order.shape, jnp.int32),
            pltpu.SMEM(kernel_map.shape, jnp.int32),
            pltpu.SMEM(halo_send.shape, jnp.int32),
            pltpu.SMEM((1, blocks), jnp.int32),
            *[pltpu.VMEM((1, width), f32)] * 6,
            pltpu.SemaphoreType.DMA((11,)),
            pltpu.VMEM((even_taps * width, channels), bf16),
            pltpu.VMEM((even_taps * width, channels), bf16),
            pltpu.VMEM(wd.shape, bf16),
            pltpu.VMEM((owners, BLK, channels), bf16),
            pltpu.VMEM((blocks, BLK, channels), bf16),
            pltpu.VMEM((2, hcap, BLK, channels), bf16),
            pltpu.VMEM((2, hcap, BLK, channels), bf16),
            pltpu.VMEM((blocks, BLK, width), bf16),
            pltpu.VMEM((n_chan - 1, blocks, BLK, width), bf16),
            pltpu.VMEM((2, hcap, BLK, width), bf16),
            pltpu.VMEM((2, n_chan, hcap, BLK, width), bf16),
            pltpu.VMEM((even_taps, blocks + 2 * hcap + 1, BLK, width), f32),
            pltpu.VMEM((wd.shape[0], blocks, cells, width), f32),
            pltpu.VMEM((blocks * cells, channels), f32),
            pltpu.VMEM((owners * slots, blocks * cells), bf16),
            pltpu.VMEM((n_chan, owners, slots, width), bf16),
            pltpu.VMEM((n_chan, owners, slots, width), bf16),
            pltpu.SemaphoreType.DMA((2 + n_chan,)),
            *pair(owners - 1),
            *pair(n_chan - 1, owners),
            *pair(2),
            *pair(n_chan - 1, groups),
            *pair(2, n_chan),
            *pair(n_chan, owners),
        ],
        compiler_params=pltpu.CompilerParams(
            collective_id=0, has_side_effects=True, vmem_limit_bytes=48 << 20
        ),
        name="encoder_level",
    )(
        features,
        scan_order,
        kernel_map,
        halo_send,
        down_route.reshape(1, blocks),
        w1.reshape(taps * width, channels),
        w2.reshape(taps * width, channels),
        wd,
        *[scale.reshape(1, width) for scale in scales],
    )


def fits(axes, features, kernel_map, width):
    n_brick, n_chan, n_sub = axes
    owners = n_brick * n_sub
    whole = width % LANES == 0 and n_chan > 1 and kernel_map.shape[0] % 4 == 0
    whole = whole and owners & (owners - 1) == 0 and n_sub & (n_sub - 1) == 0
    return whole and features.shape[0] == owners * BLK and kernel_map.shape[0] == owners * n_chan


def from_behind(block, axis, distance):
    devices = range(lax.axis_size(axis))
    route = [(i - distance, i) for i in devices if i - distance in devices]
    return lax.ppermute(block, axis, route)


def neighbours(blocks, step_by):
    return from_behind(blocks, ("brick", "sub"), step_by)


def picked(index, source):
    chosen = jnp.arange(source.shape[0], dtype=jnp.int32)[None, :] == index[:, None]
    flat = source.reshape(source.shape[0], -1)
    rows = jnp.dot(chosen.astype(source.dtype), flat, preferred_element_type=jnp.float32)
    return rows.astype(source.dtype).reshape(index.shape[0], *source.shape[1:])


def convolve(extended, weight, kernel_map):
    block_count = kernel_map.shape[0]

    def one_tap(running, inputs):
        tap_weight, index = inputs
        return running + jnp.einsum(
            "brc,dc->brd",
            picked(index, extended),
            tap_weight,
            preferred_element_type=jnp.float32,
        ), None

    initial = jnp.zeros((block_count, BLK, weight.shape[1]), jnp.float32)
    running, _ = lax.scan(one_tap, initial, (weight, kernel_map.T))
    return running


def body(
    features,
    scan_order,
    kernel_map,
    halo_send,
    down_route,
    conv1_weight,
    conv2_weight,
    down_weight,
    gain_first,
    bias_first,
    gain_second,
    bias_second,
    gain_down,
    bias_down,
):
    axes = tuple(lax.axis_size(name) for name in ("brick", "chan", "sub"))
    if fits(axes, features, kernel_map, conv1_weight.shape[1]):
        return fused(
            axes,
            features,
            scan_order,
            kernel_map,
            halo_send,
            down_route,
            conv1_weight,
            conv2_weight,
            down_weight,
            gain_first,
            bias_first,
            gain_second,
            bias_second,
            gain_down,
            bias_down,
        )
    owners = lax.axis_size(("brick", "sub"))
    per_owner = features.shape[0] // owners
    channels = features.shape[1]
    width_out = conv1_weight.shape[1]
    block_count = kernel_map.shape[0]
    channel_start = lax.axis_index("chan") * width_out
    ordered = picked(scan_order[0], features).reshape(owners, per_owner, channels)
    regrouped = lax.all_to_all(ordered, ("brick", "sub"), split_axis=0, concat_axis=0, tiled=True)
    owner_rows = lax.all_gather(regrouped, "chan", axis=1, tiled=True)
    row_blocks = owner_rows.reshape(block_count, BLK, channels)

    def extend(own):
        from_lower = neighbours(picked(halo_send[0], own), 1)
        from_upper = neighbours(picked(halo_send[1], own), -1)
        empty = jnp.zeros((1, BLK, channels), jnp.bfloat16)
        return jnp.concatenate([own, from_lower, from_upper, empty], axis=0)

    conv_first = convolve(extend(row_blocks), conv1_weight, kernel_map)
    hidden = jax.nn.relu(conv_first * gain_first + bias_first).astype(jnp.bfloat16)
    all_channels = lax.all_gather(hidden, "chan", axis=2, tiled=True)
    second = convolve(extend(all_channels), conv2_weight, kernel_map)
    residual = lax.dynamic_slice_in_dim(row_blocks, channel_start, width_out, 2)
    refined = jax.nn.relu(second * gain_second + bias_second + residual.astype(jnp.float32))
    children = refined.astype(jnp.bfloat16).reshape(block_count, 8, 8, width_out)
    partial_value = jnp.einsum(
        "oic,noqi->cnq", down_weight, children, preferred_element_type=jnp.float32
    )
    coarse = lax.psum_scatter(
        partial_value.reshape(width_out * lax.axis_size("chan"), block_count * 8).astype(
            jnp.bfloat16
        ),
        "chan",
        scatter_dimension=0,
        tiled=True,
    ).astype(jnp.float32)
    tile_values = jax.nn.relu(coarse * gain_down[:, None] + bias_down[:, None]).astype(jnp.bfloat16)
    tile_values = tile_values.reshape(width_out, block_count, 8)
    capacity = max(2, 2 * block_count // owners)
    destination = down_route[:, 0]
    number = jnp.arange(block_count, dtype=jnp.int32)
    alike = (destination[:, None] == destination[None, :]) & (number[:, None] > number[None, :])
    position = destination * capacity + jnp.sum(alike.astype(jnp.int32), axis=1)
    selector = (
        position[None, :] == jnp.arange(owners * capacity, dtype=jnp.int32)[:, None]
    ).astype(jnp.bfloat16)
    outgoing = jnp.einsum(
        "pn,cnq->cpq", selector, tile_values, preferred_element_type=jnp.float32
    ).astype(jnp.bfloat16)
    outgoing = outgoing.reshape(width_out, owners, capacity * 8)
    arrived = lax.all_to_all(outgoing, ("brick", "sub"), split_axis=1, concat_axis=2, tiled=True)
    return arrived.reshape(1, width_out, owners * capacity * 8)


def solution(mesh):
    placed = (
        P(("groups", "brick", "chan", "sub"), None),
        P(("groups", "brick", "chan", "sub"), None),
        P(("groups", "brick", "sub"), None),
        P(("groups", "brick", "sub"), None),
        P(("groups", "brick", "sub"), None),
        P(None, "chan", None),
        P(None, "chan", None),
        P(None, "chan", None),
        P("chan"),
        P("chan"),
        P("chan"),
        P("chan"),
        P("chan"),
        P("chan"),
    )
    return jax.shard_map(
        body,
        mesh=mesh,
        in_specs=placed,
        out_specs=P(("groups", "brick", "sub"), "chan", None),
        check_vma=False,
    )
```

```python
import functools

import jax
import jax.numpy as jnp
from jax import lax
from jax.experimental import pallas as pl
from jax.experimental.pallas import tpu as pltpu
from jax.sharding import PartitionSpec as P

BLK = 64
LANES = 128
MESH = pl.DeviceIdType.MESH


def products(lhs, weight, prod, place):
    width = prod.shape[3]
    shape = (lhs.shape[0] // BLK, BLK, width)

    def step(pair, carry):
        both = weight[pl.ds(pl.multiple_of(pair * 2 * width, 2 * width), 2 * width), :]
        result = lax.dot_general(
            lhs, both, (((1,), (1,)), ((), ())), preferred_element_type=jnp.float32
        )
        prod[2 * pair, place] = result[:, :width].reshape(shape)
        prod[2 * pair + 1, place] = result[:, width:].reshape(shape)
        return carry

    lax.fori_loop(0, prod.shape[0] // 2, step, 0, unroll=True)


def gathered_sum(prod, kernel_map, n):
    total = None
    for k in range(kernel_map.shape[1]):
        term = prod[k, kernel_map[n, k]]
        total = term if total is None else total + term
    return total


def flip(x, bits):
    result = x
    weight = 1
    while weight <= bits:
        if bits & weight:
            result = result + weight - 2 * weight * lax.rem(lax.div(x, weight), 2)
        weight *= 2
    return result


def fused_kernel(
    axes,
    features_hbm,
    scan_order_hbm,
    kernel_map_hbm,
    halo_send_hbm,
    down_route_hbm,
    conv1_hbm,
    conv2_hbm,
    down_hbm,
    gain_first_hbm,
    bias_first_hbm,
    gain_second_hbm,
    bias_second_hbm,
    gain_down_hbm,
    bias_down_hbm,
    out,
    features,
    scan_order,
    kernel_map,
    halo_send,
    down_route,
    gain_first,
    bias_first,
    gain_second,
    bias_second,
    gain_down,
    bias_down,
    stage_sem,
    conv1_w,
    conv2_w,
    down_w,
    ordered,
    ext,
    halo_out,
    halo_in,
    hid_own,
    hid_in,
    hid_halo_out,
    hid_halo_in,
    prod,
    kids_ref,
    part,
    selector,
    tile_out,
    tile_in,
    w_sem,
    a2a_s,
    a2a_r,
    fwd_s,
    fwd_r,
    halo_s,
    halo_r,
    hid_s,
    hid_r,
    hh_s,
    hh_r,
    tile_s,
    tile_r,
):
    staged = [
        pltpu.make_async_copy(source, place, stage_sem.at[i])
        for i, (source, place) in enumerate(
            [
                (features_hbm, features),
                (scan_order_hbm, scan_order),
                (kernel_map_hbm, kernel_map),
                (halo_send_hbm, halo_send),
                (down_route_hbm, down_route),
                (gain_first_hbm, gain_first),
                (bias_first_hbm, bias_first),
                (gain_second_hbm, gain_second),
                (bias_second_hbm, bias_second),
                (gain_down_hbm, gain_down),
                (bias_down_hbm, bias_down),
            ]
        )
    ]
    for load in staged:
        load.start()
    n_brick, n_chan, n_sub = axes
    owners = n_brick * n_sub
    blocks = kernel_map.shape[0]
    channels = features.shape[1]
    width = out.shape[1]
    hcap = halo_send.shape[1]
    group_count = hid_s.shape[1]
    group = blocks // group_count
    me_group = lax.axis_index("groups")
    chan = lax.axis_index("chan")
    me = lax.axis_index("brick") * n_sub + lax.axis_index("sub")
    own_cols = pl.ds(pl.multiple_of(chan * width, LANES), width)

    def device(owner, c):
        return (me_group, lax.div(owner, n_sub), c, lax.rem(owner, n_sub))

    def owner_at(shift):
        return lax.rem(me + shift + owners, owners)

    def chan_at(shift):
        return lax.rem(chan + shift + n_chan, n_chan)

    def remote(src, dst, send, recv, target):
        return pltpu.make_async_remote_copy(
            src_ref=src,
            dst_ref=dst,
            send_sem=send,
            recv_sem=recv,
            device_id=target,
            device_id_type=MESH,
        )

    taps = kernel_map.shape[1]
    loads = [
        pltpu.make_async_copy(conv1_hbm, conv1_w.at[pl.ds(0, taps * width)], w_sem.at[0]),
        pltpu.make_async_copy(down_hbm, down_w, w_sem.at[1]),
    ]

    def cols_from(j):
        return pl.ds(pl.multiple_of(chan_at(-j) * width, LANES), width)

    for j in range(n_chan):
        target = conv2_w.at[pl.ds(0, taps * width), pl.ds(j * width, width)]
        loads.append(
            pltpu.make_async_copy(conv2_hbm.at[:, cols_from(j)], target, w_sem.at[2 + j])
        )
    barrier = pltpu.get_barrier_semaphore()
    partners = [device(flip(me, i), chan) for i in range(1, owners)]
    partners += [device(me, chan_at(j)) for j in range(1, n_chan)]
    partners += [device(owner_at(d), chan_at(j)) for j in range(1, n_chan) for d in (1, -1)]
    for partner in partners:
        pl.semaphore_signal(barrier, inc=1, device_id=partner, device_id_type=MESH)
    for load in loads:
        load.start()

    for load in staged[:2]:
        load.wait()
    count = features.shape[0]
    source_row = lax.broadcasted_iota(jnp.int32, (count, count), 0)
    chosen = jnp.where(source_row == scan_order[...], 1.0, 0.0).astype(jnp.bfloat16)
    rows = lax.dot_general(
        chosen, features[...], (((0,), (0,)), ((), ())), preferred_element_type=jnp.float32
    ).astype(jnp.bfloat16)
    ordered[...] = rows.reshape(owners, BLK, channels)

    pl.semaphore_wait(barrier, len(partners))

    pending = []
    a2a = []
    for i in range(1, owners):
        target = flip(me, i)
        a2a.append(
            remote(
                ordered.at[target],
                ext.at[me * n_chan + chan],
                a2a_s.at[i - 1],
                a2a_r.at[i - 1],
                device(target, chan),
            )
        )
    for copy in a2a:
        copy.start()
    pending += a2a

    def forward(i, src):
        block = flip(me, i) * n_chan + chan
        for j in range(1, n_chan):
            copy = remote(
                src,
                ext.at[block],
                fwd_s.at[j - 1, i],
                fwd_r.at[j - 1, i],
                device(me, chan_at(j)),
            )
            copy.start()
            forwards[i].append(copy)

    forwards = [[] for _ in range(owners)]
    brick_blocks = n_sub * n_chan

    def pass_on(m):
        for i in range(m * n_sub, (m + 1) * n_sub):
            if i == 0:
                forward(0, ordered.at[me])
                ext[me * n_chan + chan] = ordered[me]
            else:
                a2a[i - 1].wait_recv()
                forward(i, ext.at[flip(me, i) * n_chan + chan])

    def collect(m):
        for i in range(m * n_sub, (m + 1) * n_sub):
            for copy in forwards[i]:
                copy.wait_recv()

    def multiply(m):
        place = pl.ds(flip(lax.axis_index("brick"), m) * brick_blocks, brick_blocks)
        products(ext[place].reshape(brick_blocks * BLK, channels), conv1_w, prod, place)

    pass_on(0)
    spare = conv1_w.shape[0] - taps * width
    if spare:
        conv1_w[pl.ds(taps * width, spare), :] = jnp.zeros((spare, channels), jnp.bfloat16)
        conv2_w[pl.ds(taps * width, spare), :] = jnp.zeros((spare, channels), jnp.bfloat16)
    for k in range(taps):
        prod[k, blocks + 2 * hcap] = jnp.zeros((BLK, width), jnp.float32)

    for load in staged[2:]:
        load.wait()
    slots = tile_out.shape[2]
    kids = down_w.shape[0]
    cells = BLK // kids
    capacity = slots // cells
    column = lax.broadcasted_iota(jnp.int32, (1, blocks * cells), 1)
    target_row = lax.rem(column, cells)
    names = [down_route[0, n] for n in range(blocks)]
    for n in range(blocks):
        earlier = jnp.int32(0)
        for before in range(n):
            earlier = earlier + jnp.where(names[before] == names[n], 1, 0)
        position = (names[n] * capacity + earlier) * cells
        target_row = target_row + jnp.where(lax.div(column, cells) == n, position, 0)
    slot_row = lax.broadcasted_iota(jnp.int32, (owners * slots, blocks * cells), 0)
    selector[...] = jnp.where(slot_row == target_row, 1.0, 0.0).astype(jnp.bfloat16)
    loads[0].wait()
    for m in range(1, n_brick):
        pass_on(m)
    for m in range(n_brick - 1):
        collect(m)
        multiply(m)
    collect(n_brick - 1)
    pending += [copy for copies in forwards for copy in copies]

    has_next, has_last = me < owners - 1, me > 0

    def halo_copies(direction):
        return remote(
            halo_out.at[direction],
            halo_in.at[direction],
            halo_s.at[direction],
            halo_r.at[direction],
            device(owner_at(1 if direction == 0 else -1), chan),
        )

    for direction, sends in ((0, has_next), (1, has_last)):
        for j in range(hcap):
            halo_out[direction, j] = ext[halo_send[direction, j]]
        pl.when(sends)(lambda direction=direction: halo_copies(direction).start())
    multiply(n_brick - 1)
    for direction, receives in ((0, has_last), (1, has_next)):

        @pl.when(receives)
        def _():
            halo_copies(direction).wait_recv()

        @pl.when(jnp.logical_not(receives))
        def _():
            halo_in[direction] = jnp.zeros((hcap, BLK, channels), jnp.bfloat16)

    rim = pl.ds(blocks, 2 * hcap)
    products(halo_in[...].reshape(2 * hcap * BLK, channels), conv1_w, prod, rim)

    def first_hidden(n):
        scaled = gathered_sum(prod, kernel_map, n) * gain_first[...] + bias_first[...]
        return jnp.maximum(scaled, 0.0).astype(jnp.bfloat16)

    def hid_halo_copies(direction):
        return [
            remote(
                hid_halo_out.at[direction],
                hid_halo_in.at[direction, j],
                hh_s.at[direction, j],
                hh_r.at[direction, j],
                device(owner_at(1 if direction == 0 else -1), chan_at(j)),
            )
            for j in range(n_chan)
        ]

    for direction, sends in ((0, has_next), (1, has_last)):
        for j in range(hcap):
            hid_halo_out[direction, j] = first_hidden(halo_send[direction, j])

        @pl.when(sends)
        def _():
            for copy in hid_halo_copies(direction):
                copy.start()

    hid_copies = []
    for g in range(group_count):

        def first_block(n, carry):
            hid_own[n] = first_hidden(n)
            return carry

        lax.fori_loop(g * group, (g + 1) * group, first_block, 0, unroll=2)
        place = pl.ds(g * group, group)
        for j in range(1, n_chan):
            copy = remote(
                hid_own.at[place],
                hid_in.at[j - 1, place],
                hid_s.at[j - 1, g],
                hid_r.at[j - 1, g],
                device(me, chan_at(j)),
            )
            copy.start()
            hid_copies.append(copy)
    pending += hid_copies

    for load in loads[2:]:
        load.wait()
    def second_products(g):
        place = pl.ds(g * group, group)
        halves = [hid_own[place]]
        for j in range(1, n_chan):
            hid_copies[g * (n_chan - 1) + j - 1].wait_recv()
            halves.append(hid_in[j - 1, place])
        lhs = jnp.concatenate([half.reshape(group * BLK, width) for half in halves], axis=1)
        products(lhs, conv2_w, prod, place)

    for g in range(group_count - 1):
        second_products(g)
    for direction, receives in ((0, has_last), (1, has_next)):

        @pl.when(receives)
        def _():
            for copy in hid_halo_copies(direction):
                copy.wait_recv()

        @pl.when(jnp.logical_not(receives))
        def _():
            hid_halo_in[direction] = jnp.zeros(hid_halo_in.shape[1:], jnp.bfloat16)

    halves = [hid_halo_in[:, j].reshape(2 * hcap * BLK, width) for j in range(n_chan)]
    products(jnp.concatenate(halves, axis=1), conv2_w, prod, rim)
    second_products(group_count - 1)
    loads[1].wait()

    def second_block(n, carry):
        second = gathered_sum(prod, kernel_map, n)
        residual = ext[n, :, own_cols].astype(jnp.float32)
        refined = jnp.maximum(second * gain_second[...] + bias_second[...] + residual, 0.0)
        refined = refined.reshape(kids, cells, width)
        for o in range(kids):
            kids_ref[o, n] = refined[o]
        return carry

    lax.fori_loop(0, blocks, second_block, 0, unroll=4)
    partial = None
    for o in range(kids):
        child = kids_ref[o].reshape(blocks * cells, width).astype(jnp.bfloat16)
        product = jnp.dot(child, down_w[o], preferred_element_type=jnp.float32)
        partial = product if partial is None else partial + product
    part[...] = partial
    scaled = part[:, own_cols] * gain_down[...] + bias_down[...]
    sides = [scaled.astype(jnp.bfloat16)]
    for j in range(1, n_chan):
        cols = pl.ds(pl.multiple_of(chan_at(j) * width, LANES), width)
        sides.append(part[:, cols].astype(jnp.bfloat16))
    outgoing = jnp.dot(
        selector[...], jnp.concatenate(sides, axis=1), preferred_element_type=jnp.float32
    ).astype(jnp.bfloat16)
    for j in range(n_chan):
        tile_out[j] = outgoing[:, j * width : (j + 1) * width].reshape(owners, slots, width)
    tile_copies = []
    for i in reversed(range(owners)):
        target = flip(me, i)
        for j in range(n_chan):
            if i or j:
                copy = remote(
                    tile_out.at[j, target],
                    tile_in.at[j, me],
                    tile_s.at[j, i],
                    tile_r.at[j, i],
                    device(target, chan_at(j)),
                )
                copy.start()
                tile_copies.append(copy)
    tile_in[0, me] = tile_out[0, me]
    for copy in pending:
        copy.wait_send()
    for direction, sends in ((0, has_next), (1, has_last)):

        @pl.when(sends)
        def _():
            halo_copies(direction).wait_send()
            for copy in hid_halo_copies(direction):
                copy.wait_send()

    for copy in tile_copies:
        copy.wait_recv()
    arrived = tile_in[0].reshape(owners * slots, width).astype(jnp.float32)
    for j in range(1, n_chan):
        other = tile_in[j].reshape(owners * slots, width).astype(jnp.float32)
        arrived = arrived + other * gain_down[...]
    out[0] = jnp.maximum(arrived, 0.0).T.astype(jnp.bfloat16)
    for copy in tile_copies:
        copy.wait_send()


def fused(axes, features, scan_order, kernel_map, halo_send, down_route, w1, w2, wd, *scales):
    n_brick, n_chan, n_sub = axes
    owners = n_brick * n_sub
    blocks = kernel_map.shape[0]
    channels = features.shape[1]
    width = w1.shape[1]
    hcap = halo_send.shape[1]
    taps = kernel_map.shape[1]
    even_taps = taps + taps % 2
    cells = BLK // wd.shape[0]
    slots = max(2, 2 * blocks // owners) * cells
    groups = 4
    bf16, f32 = jnp.bfloat16, jnp.float32
    vmem = pl.BlockSpec(memory_space=pltpu.VMEM)
    hbm = pl.BlockSpec(memory_space=pl.ANY)

    def pair(*shape):
        return [pltpu.SemaphoreType.DMA(shape), pltpu.SemaphoreType.DMA(shape)]

    return pl.pallas_call(
        functools.partial(fused_kernel, axes),
        out_shape=pltpu.VMEM((1, width, owners * slots), bf16),
        in_specs=[hbm] * 14,
        out_specs=vmem,
        scratch_shapes=[
            pltpu.VMEM(features.shape, bf16),
            pltpu.VMEM(scan_order.shape, jnp.int32),
            pltpu.SMEM(kernel_map.shape, jnp.int32),
            pltpu.SMEM(halo_send.shape, jnp.int32),
            pltpu.SMEM((1, blocks), jnp.int32),
            *[pltpu.VMEM((1, width), f32)] * 6,
            pltpu.SemaphoreType.DMA((11,)),
            pltpu.VMEM((even_taps * width, channels), bf16),
            pltpu.VMEM((even_taps * width, channels), bf16),
            pltpu.VMEM(wd.shape, bf16),
            pltpu.VMEM((owners, BLK, channels), bf16),
            pltpu.VMEM((blocks, BLK, channels), bf16),
            pltpu.VMEM((2, hcap, BLK, channels), bf16),
            pltpu.VMEM((2, hcap, BLK, channels), bf16),
            pltpu.VMEM((blocks, BLK, width), bf16),
            pltpu.VMEM((n_chan - 1, blocks, BLK, width), bf16),
            pltpu.VMEM((2, hcap, BLK, width), bf16),
            pltpu.VMEM((2, n_chan, hcap, BLK, width), bf16),
            pltpu.VMEM((even_taps, blocks + 2 * hcap + 1, BLK, width), f32),
            pltpu.VMEM((wd.shape[0], blocks, cells, width), f32),
            pltpu.VMEM((blocks * cells, channels), f32),
            pltpu.VMEM((owners * slots, blocks * cells), bf16),
            pltpu.VMEM((n_chan, owners, slots, width), bf16),
            pltpu.VMEM((n_chan, owners, slots, width), bf16),
            pltpu.SemaphoreType.DMA((2 + n_chan,)),
            *pair(owners - 1),
            *pair(n_chan - 1, owners),
            *pair(2),
            *pair(n_chan - 1, groups),
            *pair(2, n_chan),
            *pair(n_chan, owners),
        ],
        compiler_params=pltpu.CompilerParams(
            collective_id=0, has_side_effects=True, vmem_limit_bytes=66977792
        ),
        name="encoder_level",
    )(
        features,
        scan_order,
        kernel_map,
        halo_send,
        down_route.reshape(1, blocks),
        w1.reshape(taps * width, channels),
        w2.reshape(taps * width, channels),
        wd,
        *[scale.reshape(1, width) for scale in scales],
    )


def fits(axes, features, kernel_map, width):
    n_brick, n_chan, n_sub = axes
    owners = n_brick * n_sub
    whole = width % LANES == 0 and n_chan > 1 and kernel_map.shape[0] % 4 == 0
    whole = whole and owners & (owners - 1) == 0 and n_sub & (n_sub - 1) == 0
    return whole and features.shape[0] == owners * BLK and kernel_map.shape[0] == owners * n_chan


def from_behind(block, axis, distance):
    devices = range(lax.axis_size(axis))
    route = [(i - distance, i) for i in devices if i - distance in devices]
    return lax.ppermute(block, axis, route)


def neighbours(blocks, step_by):
    return from_behind(blocks, ("brick", "sub"), step_by)


def picked(index, source):
    chosen = jnp.arange(source.shape[0], dtype=jnp.int32)[None, :] == index[:, None]
    flat = source.reshape(source.shape[0], -1)
    rows = jnp.dot(chosen.astype(source.dtype), flat, preferred_element_type=jnp.float32)
    return rows.astype(source.dtype).reshape(index.shape[0], *source.shape[1:])


def convolve(extended, weight, kernel_map):
    block_count = kernel_map.shape[0]

    def one_tap(running, inputs):
        tap_weight, index = inputs
        return running + jnp.einsum(
            "brc,dc->brd",
            picked(index, extended),
            tap_weight,
            preferred_element_type=jnp.float32,
        ), None

    initial = jnp.zeros((block_count, BLK, weight.shape[1]), jnp.float32)
    running, _ = lax.scan(one_tap, initial, (weight, kernel_map.T))
    return running


def body(
    features,
    scan_order,
    kernel_map,
    halo_send,
    down_route,
    conv1_weight,
    conv2_weight,
    down_weight,
    gain_first,
    bias_first,
    gain_second,
    bias_second,
    gain_down,
    bias_down,
):
    axes = tuple(lax.axis_size(name) for name in ("brick", "chan", "sub"))
    if fits(axes, features, kernel_map, conv1_weight.shape[1]):
        return fused(
            axes,
            features,
            scan_order,
            kernel_map,
            halo_send,
            down_route,
            conv1_weight,
            conv2_weight,
            down_weight,
            gain_first,
            bias_first,
            gain_second,
            bias_second,
            gain_down,
            bias_down,
        )
    owners = lax.axis_size(("brick", "sub"))
    per_owner = features.shape[0] // owners
    channels = features.shape[1]
    width_out = conv1_weight.shape[1]
    block_count = kernel_map.shape[0]
    channel_start = lax.axis_index("chan") * width_out
    ordered = picked(scan_order[0], features).reshape(owners, per_owner, channels)
    regrouped = lax.all_to_all(ordered, ("brick", "sub"), split_axis=0, concat_axis=0, tiled=True)
    owner_rows = lax.all_gather(regrouped, "chan", axis=1, tiled=True)
    row_blocks = owner_rows.reshape(block_count, BLK, channels)

    def extend(own):
        from_lower = neighbours(picked(halo_send[0], own), 1)
        from_upper = neighbours(picked(halo_send[1], own), -1)
        empty = jnp.zeros((1, BLK, channels), jnp.bfloat16)
        return jnp.concatenate([own, from_lower, from_upper, empty], axis=0)

    conv_first = convolve(extend(row_blocks), conv1_weight, kernel_map)
    hidden = jax.nn.relu(conv_first * gain_first + bias_first).astype(jnp.bfloat16)
    all_channels = lax.all_gather(hidden, "chan", axis=2, tiled=True)
    second = convolve(extend(all_channels), conv2_weight, kernel_map)
    residual = lax.dynamic_slice_in_dim(row_blocks, channel_start, width_out, 2)
    refined = jax.nn.relu(second * gain_second + bias_second + residual.astype(jnp.float32))
    children = refined.astype(jnp.bfloat16).reshape(block_count, 8, 8, width_out)
    partial_value = jnp.einsum(
        "oic,noqi->cnq", down_weight, children, preferred_element_type=jnp.float32
    )
    coarse = lax.psum_scatter(
        partial_value.reshape(width_out * lax.axis_size("chan"), block_count * 8).astype(
            jnp.bfloat16
        ),
        "chan",
        scatter_dimension=0,
        tiled=True,
    ).astype(jnp.float32)
    tile_values = jax.nn.relu(coarse * gain_down[:, None] + bias_down[:, None]).astype(jnp.bfloat16)
    tile_values = tile_values.reshape(width_out, block_count, 8)
    capacity = max(2, 2 * block_count // owners)
    destination = down_route[:, 0]
    number = jnp.arange(block_count, dtype=jnp.int32)
    alike = (destination[:, None] == destination[None, :]) & (number[:, None] > number[None, :])
    position = destination * capacity + jnp.sum(alike.astype(jnp.int32), axis=1)
    selector = (
        position[None, :] == jnp.arange(owners * capacity, dtype=jnp.int32)[:, None]
    ).astype(jnp.bfloat16)
    outgoing = jnp.einsum(
        "pn,cnq->cpq", selector, tile_values, preferred_element_type=jnp.float32
    ).astype(jnp.bfloat16)
    outgoing = outgoing.reshape(width_out, owners, capacity * 8)
    arrived = lax.all_to_all(outgoing, ("brick", "sub"), split_axis=1, concat_axis=2, tiled=True)
    return arrived.reshape(1, width_out, owners * capacity * 8)


def solution(mesh):
    placed = (
        P(("groups", "brick", "chan", "sub"), None),
        P(("groups", "brick", "chan", "sub"), None),
        P(("groups", "brick", "sub"), None),
        P(("groups", "brick", "sub"), None),
        P(("groups", "brick", "sub"), None),
        P(None, "chan", None),
        P(None, "chan", None),
        P(None, "chan", None),
        P("chan"),
        P("chan"),
        P("chan"),
        P("chan"),
        P("chan"),
        P("chan"),
    )
    return jax.shard_map(
        body,
        mesh=mesh,
        in_specs=placed,
        out_specs=P(("groups", "brick", "sub"), "chan", None),
        check_vma=False,
    )
```

```python
import functools

import jax
import jax.numpy as jnp
from jax import lax
from jax.experimental import pallas as pl
from jax.experimental.pallas import tpu as pltpu
from jax.sharding import PartitionSpec as P

BLK = 64
LANES = 128
MESH = pl.DeviceIdType.MESH


def products(lhs, weight, prod, place):
    width = prod.shape[3]
    shape = (lhs.shape[0] // BLK, BLK, width)

    def step(pair, carry):
        both = weight[pl.ds(pl.multiple_of(pair * 2 * width, 2 * width), 2 * width), :]
        result = lax.dot_general(
            lhs, both, (((1,), (1,)), ((), ())), preferred_element_type=jnp.float32
        )
        prod[2 * pair, place] = result[:, :width].reshape(shape)
        prod[2 * pair + 1, place] = result[:, width:].reshape(shape)
        return carry

    lax.fori_loop(0, prod.shape[0] // 2, step, 0, unroll=True)


def gathered_sum(prod, kernel_map, n):
    total = None
    for k in range(kernel_map.shape[1]):
        term = prod[k, kernel_map[n, k]]
        total = term if total is None else total + term
    return total


def flip(x, bits):
    result = x
    weight = 1
    while weight <= bits:
        if bits & weight:
            result = result + weight - 2 * weight * lax.rem(lax.div(x, weight), 2)
        weight *= 2
    return result


def fused_kernel(
    axes,
    features_hbm,
    scan_order_hbm,
    kernel_map_hbm,
    halo_send_hbm,
    down_route_hbm,
    conv1_hbm,
    conv2_hbm,
    down_hbm,
    gain_first_hbm,
    bias_first_hbm,
    gain_second_hbm,
    bias_second_hbm,
    gain_down_hbm,
    bias_down_hbm,
    out,
    features,
    scan_order,
    kernel_map,
    halo_send,
    down_route,
    gain_first,
    bias_first,
    gain_second,
    bias_second,
    gain_down,
    bias_down,
    stage_sem,
    conv1_w,
    conv2_w,
    down_w,
    ordered,
    ext,
    halo_out,
    halo_in,
    hid_own,
    hid_in,
    hid_halo_out,
    hid_halo_in,
    prod,
    kids_ref,
    part,
    selector,
    tile_out,
    tile_in,
    w_sem,
    a2a_s,
    a2a_r,
    fwd_s,
    fwd_r,
    halo_s,
    halo_r,
    hid_s,
    hid_r,
    hh_s,
    hh_r,
    tile_s,
    tile_r,
):
    staged = [
        pltpu.make_async_copy(source, place, stage_sem.at[i])
        for i, (source, place) in enumerate(
            [
                (features_hbm, features),
                (scan_order_hbm, scan_order),
                (kernel_map_hbm, kernel_map),
                (halo_send_hbm, halo_send),
                (down_route_hbm, down_route),
                (gain_first_hbm, gain_first),
                (bias_first_hbm, bias_first),
                (gain_second_hbm, gain_second),
                (bias_second_hbm, bias_second),
                (gain_down_hbm, gain_down),
                (bias_down_hbm, bias_down),
            ]
        )
    ]
    for load in staged:
        load.start()
    n_brick, n_chan, n_sub = axes
    owners = n_brick * n_sub
    blocks = kernel_map.shape[0]
    channels = features.shape[1]
    width = out.shape[1]
    hcap = halo_send.shape[1]
    group_count = hid_s.shape[1]
    group = blocks // group_count
    me_group = lax.axis_index("groups")
    chan = lax.axis_index("chan")
    me = lax.axis_index("brick") * n_sub + lax.axis_index("sub")
    own_cols = pl.ds(pl.multiple_of(chan * width, LANES), width)

    def device(owner, c):
        return (me_group, lax.div(owner, n_sub), c, lax.rem(owner, n_sub))

    def owner_at(shift):
        return lax.rem(me + shift + owners, owners)

    def chan_at(shift):
        return lax.rem(chan + shift + n_chan, n_chan)

    def remote(src, dst, send, recv, target):
        return pltpu.make_async_remote_copy(
            src_ref=src,
            dst_ref=dst,
            send_sem=send,
            recv_sem=recv,
            device_id=target,
            device_id_type=MESH,
        )

    taps = kernel_map.shape[1]
    loads = [
        pltpu.make_async_copy(conv1_hbm, conv1_w.at[pl.ds(0, taps * width)], w_sem.at[0]),
        pltpu.make_async_copy(down_hbm, down_w, w_sem.at[1]),
    ]

    def cols_from(j):
        return pl.ds(pl.multiple_of(chan_at(-j) * width, LANES), width)

    for j in range(n_chan):
        target = conv2_w.at[pl.ds(0, taps * width), pl.ds(j * width, width)]
        loads.append(
            pltpu.make_async_copy(conv2_hbm.at[:, cols_from(j)], target, w_sem.at[2 + j])
        )
    barrier = pltpu.get_barrier_semaphore()
    partners = [device(flip(me, i), chan) for i in range(1, owners)]
    partners += [device(me, chan_at(j)) for j in range(1, n_chan)]
    partners += [device(owner_at(d), chan_at(j)) for j in range(1, n_chan) for d in (1, -1)]
    for partner in partners:
        pl.semaphore_signal(barrier, inc=1, device_id=partner, device_id_type=MESH)
    for load in loads:
        load.start()

    for load in staged[:2]:
        load.wait()
    count = features.shape[0]
    source_row = lax.broadcasted_iota(jnp.int32, (count, count), 0)
    chosen = jnp.where(source_row == scan_order[...], 1.0, 0.0).astype(jnp.bfloat16)
    rows = lax.dot_general(
        chosen, features[...], (((0,), (0,)), ((), ())), preferred_element_type=jnp.float32
    ).astype(jnp.bfloat16)
    ordered[...] = rows.reshape(owners, BLK, channels)

    pl.semaphore_wait(barrier, len(partners))

    pending = []
    a2a = []
    for i in range(1, owners):
        target = flip(me, i)
        a2a.append(
            remote(
                ordered.at[target],
                ext.at[me * n_chan + chan],
                a2a_s.at[i - 1],
                a2a_r.at[i - 1],
                device(target, chan),
            )
        )
    for copy in a2a:
        copy.start()
    pending += a2a

    def forward(i, src):
        block = flip(me, i) * n_chan + chan
        for j in range(1, n_chan):
            copy = remote(
                src,
                ext.at[block],
                fwd_s.at[j - 1, i],
                fwd_r.at[j - 1, i],
                device(me, chan_at(j)),
            )
            copy.start()
            forwards[i].append(copy)

    forwards = [[] for _ in range(owners)]
    brick_blocks = n_sub * n_chan

    def pass_on(m):
        for i in range(m * n_sub, (m + 1) * n_sub):
            if i == 0:
                forward(0, ordered.at[me])
                ext[me * n_chan + chan] = ordered[me]
            else:
                a2a[i - 1].wait_recv()
                forward(i, ext.at[flip(me, i) * n_chan + chan])

    def collect(m):
        for i in range(m * n_sub, (m + 1) * n_sub):
            for copy in forwards[i]:
                copy.wait_recv()

    def multiply(m):
        place = pl.ds(flip(lax.axis_index("brick"), m) * brick_blocks, brick_blocks)
        products(ext[place].reshape(brick_blocks * BLK, channels), conv1_w, prod, place)

    pass_on(0)
    spare = conv1_w.shape[0] - taps * width
    if spare:
        conv1_w[pl.ds(taps * width, spare), :] = jnp.zeros((spare, channels), jnp.bfloat16)
        conv2_w[pl.ds(taps * width, spare), :] = jnp.zeros((spare, channels), jnp.bfloat16)
    for k in range(taps):
        prod[k, blocks + 2 * hcap] = jnp.zeros((BLK, width), jnp.float32)

    for load in staged[2:]:
        load.wait()
    slots = tile_out.shape[2]
    kids = down_w.shape[0]
    cells = BLK // kids
    capacity = slots // cells
    column = lax.broadcasted_iota(jnp.int32, (1, blocks * cells), 1)
    target_row = lax.rem(column, cells)
    names = [down_route[0, n] for n in range(blocks)]
    for n in range(blocks):
        earlier = jnp.int32(0)
        for before in range(n):
            earlier = earlier + jnp.where(names[before] == names[n], 1, 0)
        position = (names[n] * capacity + earlier) * cells
        target_row = target_row + jnp.where(lax.div(column, cells) == n, position, 0)
    slot_row = lax.broadcasted_iota(jnp.int32, (owners * slots, blocks * cells), 0)
    selector[...] = jnp.where(slot_row == target_row, 1.0, 0.0).astype(jnp.bfloat16)
    loads[0].wait()
    for m in range(1, n_brick):
        pass_on(m)
    for m in range(n_brick - 1):
        collect(m)
        multiply(m)
    collect(n_brick - 1)
    pending += [copy for copies in forwards for copy in copies]

    has_next, has_last = me < owners - 1, me > 0

    def halo_copies(direction):
        return remote(
            halo_out.at[direction],
            halo_in.at[direction],
            halo_s.at[direction],
            halo_r.at[direction],
            device(owner_at(1 if direction == 0 else -1), chan),
        )

    for direction, sends in ((0, has_next), (1, has_last)):
        for j in range(hcap):
            halo_out[direction, j] = ext[halo_send[direction, j]]
        pl.when(sends)(lambda direction=direction: halo_copies(direction).start())
    multiply(n_brick - 1)
    for direction, receives in ((0, has_last), (1, has_next)):

        @pl.when(receives)
        def _():
            halo_copies(direction).wait_recv()

        @pl.when(jnp.logical_not(receives))
        def _():
            halo_in[direction] = jnp.zeros((hcap, BLK, channels), jnp.bfloat16)

    rim = pl.ds(blocks, 2 * hcap)
    products(halo_in[...].reshape(2 * hcap * BLK, channels), conv1_w, prod, rim)

    def first_hidden(n):
        scaled = gathered_sum(prod, kernel_map, n) * gain_first[...] + bias_first[...]
        return jnp.maximum(scaled, 0.0).astype(jnp.bfloat16)

    def hid_halo_copies(direction):
        return [
            remote(
                hid_halo_out.at[direction],
                hid_halo_in.at[direction, j],
                hh_s.at[direction, j],
                hh_r.at[direction, j],
                device(owner_at(1 if direction == 0 else -1), chan_at(j)),
            )
            for j in range(n_chan)
        ]

    for direction, sends in ((0, has_next), (1, has_last)):
        for j in range(hcap):
            hid_halo_out[direction, j] = first_hidden(halo_send[direction, j])

        @pl.when(sends)
        def _():
            for copy in hid_halo_copies(direction):
                copy.start()

    hid_copies = []
    for g in range(group_count):

        def first_block(n, carry):
            hid_own[n] = first_hidden(n)
            return carry

        lax.fori_loop(g * group, (g + 1) * group, first_block, 0, unroll=2)
        place = pl.ds(g * group, group)
        for j in range(1, n_chan):
            copy = remote(
                hid_own.at[place],
                hid_in.at[j - 1, place],
                hid_s.at[j - 1, g],
                hid_r.at[j - 1, g],
                device(me, chan_at(j)),
            )
            copy.start()
            hid_copies.append(copy)
    pending += hid_copies

    for load in loads[2:]:
        load.wait()
    def second_products(g):
        place = pl.ds(g * group, group)
        halves = [hid_own[place]]
        for j in range(1, n_chan):
            hid_copies[g * (n_chan - 1) + j - 1].wait_recv()
            halves.append(hid_in[j - 1, place])
        lhs = jnp.concatenate([half.reshape(group * BLK, width) for half in halves], axis=1)
        products(lhs, conv2_w, prod, place)

    for g in range(group_count - 1):
        second_products(g)
    for direction, receives in ((0, has_last), (1, has_next)):

        @pl.when(receives)
        def _():
            for copy in hid_halo_copies(direction):
                copy.wait_recv()

        @pl.when(jnp.logical_not(receives))
        def _():
            hid_halo_in[direction] = jnp.zeros(hid_halo_in.shape[1:], jnp.bfloat16)

    halves = [hid_halo_in[:, j].reshape(2 * hcap * BLK, width) for j in range(n_chan)]
    products(jnp.concatenate(halves, axis=1), conv2_w, prod, rim)
    second_products(group_count - 1)
    loads[1].wait()

    def second_block(n, carry):
        second = gathered_sum(prod, kernel_map, n)
        residual = ext[n, :, own_cols].astype(jnp.float32)
        refined = jnp.maximum(second * gain_second[...] + bias_second[...] + residual, 0.0)
        refined = refined.reshape(kids, cells, width)
        for o in range(kids):
            kids_ref[o, n] = refined[o]
        return carry

    lax.fori_loop(0, blocks, second_block, 0, unroll=4)
    partial = None
    for o in range(kids):
        child = kids_ref[o].reshape(blocks * cells, width).astype(jnp.bfloat16)
        product = jnp.dot(child, down_w[o], preferred_element_type=jnp.float32)
        partial = product if partial is None else partial + product
    part[...] = partial
    scaled = part[:, own_cols] * gain_down[...] + bias_down[...]
    sides = [scaled.astype(jnp.bfloat16)]
    for j in range(1, n_chan):
        cols = pl.ds(pl.multiple_of(chan_at(j) * width, LANES), width)
        sides.append(part[:, cols].astype(jnp.bfloat16))
    outgoing = jnp.dot(
        selector[...], jnp.concatenate(sides, axis=1), preferred_element_type=jnp.float32
    ).astype(jnp.bfloat16)
    for j in range(n_chan):
        tile_out[j] = outgoing[:, j * width : (j + 1) * width].reshape(owners, slots, width)
    def tile_copy(j, target, source):
        return remote(
            tile_out.at[j, target],
            tile_in.at[j, source],
            tile_s.at[j, target],
            tile_r.at[j, source],
            device(target, chan_at(j)),
        )

    def tile_copies(act):
        for other in [*range(n_sub), *reversed(range(n_sub, owners))]:
            for j in reversed(range(n_chan)):
                if j:
                    act(j, other)
                else:
                    pl.when(me != other)(functools.partial(act, j, other))

    tile_copies(lambda j, other: tile_copy(j, other, me).start())
    tile_in[0, me] = tile_out[0, me]
    for copy in pending:
        copy.wait_send()
    for direction, sends in ((0, has_next), (1, has_last)):

        @pl.when(sends)
        def _():
            halo_copies(direction).wait_send()
            for copy in hid_halo_copies(direction):
                copy.wait_send()

    tile_copies(lambda j, other: tile_copy(j, other, other).wait_recv())
    arrived = tile_in[0].reshape(owners * slots, width).astype(jnp.float32)
    for j in range(1, n_chan):
        other = tile_in[j].reshape(owners * slots, width).astype(jnp.float32)
        arrived = arrived + other * gain_down[...]
    out[0] = jnp.maximum(arrived, 0.0).T.astype(jnp.bfloat16)
    tile_copies(lambda j, other: tile_copy(j, other, other).wait_send())


def fused(axes, features, scan_order, kernel_map, halo_send, down_route, w1, w2, wd, *scales):
    n_brick, n_chan, n_sub = axes
    owners = n_brick * n_sub
    blocks = kernel_map.shape[0]
    channels = features.shape[1]
    width = w1.shape[1]
    hcap = halo_send.shape[1]
    taps = kernel_map.shape[1]
    even_taps = taps + taps % 2
    cells = BLK // wd.shape[0]
    slots = max(2, 2 * blocks // owners) * cells
    groups = 4
    bf16, f32 = jnp.bfloat16, jnp.float32
    vmem = pl.BlockSpec(memory_space=pltpu.VMEM)
    hbm = pl.BlockSpec(memory_space=pl.ANY)

    def pair(*shape):
        return [pltpu.SemaphoreType.DMA(shape), pltpu.SemaphoreType.DMA(shape)]

    return pl.pallas_call(
        functools.partial(fused_kernel, axes),
        out_shape=pltpu.VMEM((1, width, owners * slots), bf16),
        in_specs=[hbm] * 14,
        out_specs=vmem,
        scratch_shapes=[
            pltpu.VMEM(features.shape, bf16),
            pltpu.VMEM(scan_order.shape, jnp.int32),
            pltpu.SMEM(kernel_map.shape, jnp.int32),
            pltpu.SMEM(halo_send.shape, jnp.int32),
            pltpu.SMEM((1, blocks), jnp.int32),
            *[pltpu.VMEM((1, width), f32)] * 6,
            pltpu.SemaphoreType.DMA((11,)),
            pltpu.VMEM((even_taps * width, channels), bf16),
            pltpu.VMEM((even_taps * width, channels), bf16),
            pltpu.VMEM(wd.shape, bf16),
            pltpu.VMEM((owners, BLK, channels), bf16),
            pltpu.VMEM((blocks, BLK, channels), bf16),
            pltpu.VMEM((2, hcap, BLK, channels), bf16),
            pltpu.VMEM((2, hcap, BLK, channels), bf16),
            pltpu.VMEM((blocks, BLK, width), bf16),
            pltpu.VMEM((n_chan - 1, blocks, BLK, width), bf16),
            pltpu.VMEM((2, hcap, BLK, width), bf16),
            pltpu.VMEM((2, n_chan, hcap, BLK, width), bf16),
            pltpu.VMEM((even_taps, blocks + 2 * hcap + 1, BLK, width), f32),
            pltpu.VMEM((wd.shape[0], blocks, cells, width), f32),
            pltpu.VMEM((blocks * cells, channels), f32),
            pltpu.VMEM((owners * slots, blocks * cells), bf16),
            pltpu.VMEM((n_chan, owners, slots, width), bf16),
            pltpu.VMEM((n_chan, owners, slots, width), bf16),
            pltpu.SemaphoreType.DMA((2 + n_chan,)),
            *pair(owners - 1),
            *pair(n_chan - 1, owners),
            *pair(2),
            *pair(n_chan - 1, groups),
            *pair(2, n_chan),
            *pair(n_chan, owners),
        ],
        compiler_params=pltpu.CompilerParams(
            collective_id=0, has_side_effects=True, vmem_limit_bytes=66977792
        ),
        name="encoder_level",
    )(
        features,
        scan_order,
        kernel_map,
        halo_send,
        down_route.reshape(1, blocks),
        w1.reshape(taps * width, channels),
        w2.reshape(taps * width, channels),
        wd,
        *[scale.reshape(1, width) for scale in scales],
    )


def fits(axes, features, kernel_map, width):
    n_brick, n_chan, n_sub = axes
    owners = n_brick * n_sub
    whole = width % LANES == 0 and n_chan > 1 and kernel_map.shape[0] % 4 == 0
    whole = whole and owners & (owners - 1) == 0 and n_sub & (n_sub - 1) == 0
    return whole and features.shape[0] == owners * BLK and kernel_map.shape[0] == owners * n_chan


def from_behind(block, axis, distance):
    devices = range(lax.axis_size(axis))
    route = [(i - distance, i) for i in devices if i - distance in devices]
    return lax.ppermute(block, axis, route)


def neighbours(blocks, step_by):
    return from_behind(blocks, ("brick", "sub"), step_by)


def picked(index, source):
    chosen = jnp.arange(source.shape[0], dtype=jnp.int32)[None, :] == index[:, None]
    flat = source.reshape(source.shape[0], -1)
    rows = jnp.dot(chosen.astype(source.dtype), flat, preferred_element_type=jnp.float32)
    return rows.astype(source.dtype).reshape(index.shape[0], *source.shape[1:])


def convolve(extended, weight, kernel_map):
    block_count = kernel_map.shape[0]

    def one_tap(running, inputs):
        tap_weight, index = inputs
        return running + jnp.einsum(
            "brc,dc->brd",
            picked(index, extended),
            tap_weight,
            preferred_element_type=jnp.float32,
        ), None

    initial = jnp.zeros((block_count, BLK, weight.shape[1]), jnp.float32)
    running, _ = lax.scan(one_tap, initial, (weight, kernel_map.T))
    return running


def body(
    features,
    scan_order,
    kernel_map,
    halo_send,
    down_route,
    conv1_weight,
    conv2_weight,
    down_weight,
    gain_first,
    bias_first,
    gain_second,
    bias_second,
    gain_down,
    bias_down,
):
    axes = tuple(lax.axis_size(name) for name in ("brick", "chan", "sub"))
    if fits(axes, features, kernel_map, conv1_weight.shape[1]):
        return fused(
            axes,
            features,
            scan_order,
            kernel_map,
            halo_send,
            down_route,
            conv1_weight,
            conv2_weight,
            down_weight,
            gain_first,
            bias_first,
            gain_second,
            bias_second,
            gain_down,
            bias_down,
        )
    owners = lax.axis_size(("brick", "sub"))
    per_owner = features.shape[0] // owners
    channels = features.shape[1]
    width_out = conv1_weight.shape[1]
    block_count = kernel_map.shape[0]
    channel_start = lax.axis_index("chan") * width_out
    ordered = picked(scan_order[0], features).reshape(owners, per_owner, channels)
    regrouped = lax.all_to_all(ordered, ("brick", "sub"), split_axis=0, concat_axis=0, tiled=True)
    owner_rows = lax.all_gather(regrouped, "chan", axis=1, tiled=True)
    row_blocks = owner_rows.reshape(block_count, BLK, channels)

    def extend(own):
        from_lower = neighbours(picked(halo_send[0], own), 1)
        from_upper = neighbours(picked(halo_send[1], own), -1)
        empty = jnp.zeros((1, BLK, channels), jnp.bfloat16)
        return jnp.concatenate([own, from_lower, from_upper, empty], axis=0)

    conv_first = convolve(extend(row_blocks), conv1_weight, kernel_map)
    hidden = jax.nn.relu(conv_first * gain_first + bias_first).astype(jnp.bfloat16)
    all_channels = lax.all_gather(hidden, "chan", axis=2, tiled=True)
    second = convolve(extend(all_channels), conv2_weight, kernel_map)
    residual = lax.dynamic_slice_in_dim(row_blocks, channel_start, width_out, 2)
    refined = jax.nn.relu(second * gain_second + bias_second + residual.astype(jnp.float32))
    children = refined.astype(jnp.bfloat16).reshape(block_count, 8, 8, width_out)
    partial_value = jnp.einsum(
        "oic,noqi->cnq", down_weight, children, preferred_element_type=jnp.float32
    )
    coarse = lax.psum_scatter(
        partial_value.reshape(width_out * lax.axis_size("chan"), block_count * 8).astype(
            jnp.bfloat16
        ),
        "chan",
        scatter_dimension=0,
        tiled=True,
    ).astype(jnp.float32)
    tile_values = jax.nn.relu(coarse * gain_down[:, None] + bias_down[:, None]).astype(jnp.bfloat16)
    tile_values = tile_values.reshape(width_out, block_count, 8)
    capacity = max(2, 2 * block_count // owners)
    destination = down_route[:, 0]
    number = jnp.arange(block_count, dtype=jnp.int32)
    alike = (destination[:, None] == destination[None, :]) & (number[:, None] > number[None, :])
    position = destination * capacity + jnp.sum(alike.astype(jnp.int32), axis=1)
    selector = (
        position[None, :] == jnp.arange(owners * capacity, dtype=jnp.int32)[:, None]
    ).astype(jnp.bfloat16)
    outgoing = jnp.einsum(
        "pn,cnq->cpq", selector, tile_values, preferred_element_type=jnp.float32
    ).astype(jnp.bfloat16)
    outgoing = outgoing.reshape(width_out, owners, capacity * 8)
    arrived = lax.all_to_all(outgoing, ("brick", "sub"), split_axis=1, concat_axis=2, tiled=True)
    return arrived.reshape(1, width_out, owners * capacity * 8)


def solution(mesh):
    placed = (
        P(("groups", "brick", "chan", "sub"), None),
        P(("groups", "brick", "chan", "sub"), None),
        P(("groups", "brick", "sub"), None),
        P(("groups", "brick", "sub"), None),
        P(("groups", "brick", "sub"), None),
        P(None, "chan", None),
        P(None, "chan", None),
        P(None, "chan", None),
        P("chan"),
        P("chan"),
        P("chan"),
        P("chan"),
        P("chan"),
        P("chan"),
    )
    return jax.shard_map(
        body,
        mesh=mesh,
        in_specs=placed,
        out_specs=P(("groups", "brick", "sub"), "chan", None),
        check_vma=False,
    )
```

```python
import functools

import jax
import jax.numpy as jnp
from jax import lax
from jax.experimental import pallas as pl
from jax.experimental.pallas import tpu as pltpu
from jax.sharding import PartitionSpec as P

BLK = 64
LANES = 128
MESH = pl.DeviceIdType.MESH


def products(lhs, weight, prod, place):
    width = prod.shape[3]
    shape = (lhs.shape[0] // BLK, BLK, width)

    def step(pair, carry):
        both = weight[pl.ds(pl.multiple_of(pair * 2 * width, 2 * width), 2 * width), :]
        result = lax.dot_general(
            lhs, both, (((1,), (1,)), ((), ())), preferred_element_type=jnp.float32
        )
        prod[2 * pair, place] = result[:, :width].reshape(shape)
        prod[2 * pair + 1, place] = result[:, width:].reshape(shape)
        return carry

    lax.fori_loop(0, prod.shape[0] // 2, step, 0, unroll=True)


def gathered_sum(prod, kernel_map, n):
    total = None
    for k in range(kernel_map.shape[1]):
        term = prod[k, kernel_map[n, k]]
        total = term if total is None else total + term
    return total


def flip(x, bits):
    result = x
    weight = 1
    while weight <= bits:
        if bits & weight:
            result = result + weight - 2 * weight * lax.rem(lax.div(x, weight), 2)
        weight *= 2
    return result


def fused_kernel(
    axes,
    features_hbm,
    scan_order_hbm,
    kernel_map_hbm,
    halo_send_hbm,
    down_route_hbm,
    conv1_hbm,
    conv2_hbm,
    down_hbm,
    gain_first_hbm,
    bias_first_hbm,
    gain_second_hbm,
    bias_second_hbm,
    gain_down_hbm,
    bias_down_hbm,
    out,
    features,
    scan_order,
    kernel_map,
    halo_send,
    down_route,
    gain_first,
    bias_first,
    gain_second,
    bias_second,
    gain_down,
    bias_down,
    stage_sem,
    conv1_w,
    conv2_w,
    down_w,
    ordered,
    ext,
    halo_out,
    halo_in,
    hid_own,
    hid_in,
    hid_halo_out,
    hid_halo_in,
    prod,
    kids_ref,
    selector,
    tile_out,
    tile_in,
    w_sem,
    a2a_s,
    a2a_r,
    fwd_s,
    fwd_r,
    halo_s,
    halo_r,
    hid_s,
    hid_r,
    hh_s,
    hh_r,
    tile_s,
    tile_r,
):
    staged = [
        pltpu.make_async_copy(source, place, stage_sem.at[i])
        for i, (source, place) in enumerate(
            [
                (features_hbm, features),
                (scan_order_hbm, scan_order),
                (kernel_map_hbm, kernel_map),
                (halo_send_hbm, halo_send),
                (down_route_hbm, down_route),
                (gain_first_hbm, gain_first),
                (bias_first_hbm, bias_first),
                (gain_second_hbm, gain_second),
                (bias_second_hbm, bias_second),
                (gain_down_hbm, gain_down),
                (bias_down_hbm, bias_down),
            ]
        )
    ]
    for load in staged:
        load.start()
    n_brick, n_chan, n_sub = axes
    owners = n_brick * n_sub
    blocks = kernel_map.shape[0]
    channels = features.shape[1]
    width = out.shape[1]
    hcap = halo_send.shape[1]
    group_count = hid_s.shape[1]
    group = blocks // group_count
    me_group = lax.axis_index("groups")
    chan = lax.axis_index("chan")
    me = lax.axis_index("brick") * n_sub + lax.axis_index("sub")
    own_cols = pl.ds(pl.multiple_of(chan * width, LANES), width)

    def device(owner, c):
        return (me_group, lax.div(owner, n_sub), c, lax.rem(owner, n_sub))

    def owner_at(shift):
        return lax.rem(me + shift + owners, owners)

    def chan_at(shift):
        return lax.rem(chan + shift + n_chan, n_chan)

    def remote(src, dst, send, recv, target):
        return pltpu.make_async_remote_copy(
            src_ref=src,
            dst_ref=dst,
            send_sem=send,
            recv_sem=recv,
            device_id=target,
            device_id_type=MESH,
        )

    taps = kernel_map.shape[1]
    loads = [
        pltpu.make_async_copy(conv1_hbm, conv1_w.at[pl.ds(0, taps * width)], w_sem.at[0]),
        pltpu.make_async_copy(down_hbm, down_w, w_sem.at[1]),
    ]

    def cols_from(j):
        return pl.ds(pl.multiple_of(chan_at(-j) * width, LANES), width)

    for j in range(n_chan):
        target = conv2_w.at[pl.ds(0, taps * width), pl.ds(j * width, width)]
        loads.append(
            pltpu.make_async_copy(conv2_hbm.at[:, cols_from(j)], target, w_sem.at[2 + j])
        )
    barrier = pltpu.get_barrier_semaphore()
    partners = [device(flip(me, i), chan) for i in reversed(range(1, owners))]
    partners += [device(me, chan_at(j)) for j in range(1, n_chan)]
    for partner in partners:
        pl.semaphore_signal(barrier, inc=1, device_id=partner, device_id_type=MESH)
    for load in loads:
        load.start()

    for load in staged[:2]:
        load.wait()
    count = features.shape[0]
    source_row = lax.broadcasted_iota(jnp.int32, (count, count), 0)
    chosen = jnp.where(source_row == scan_order[...], 1.0, 0.0).astype(jnp.bfloat16)
    rows = lax.dot_general(
        chosen, features[...], (((0,), (0,)), ((), ())), preferred_element_type=jnp.float32
    ).astype(jnp.bfloat16)
    ordered[...] = rows.reshape(owners, BLK, channels)

    pl.semaphore_wait(barrier, len(partners))

    pending = []
    a2a = []
    for i in range(1, owners):
        target = flip(me, i)
        a2a.append(
            remote(
                ordered.at[target],
                ext.at[me * n_chan + chan],
                a2a_s.at[i - 1],
                a2a_r.at[i - 1],
                device(target, chan),
            )
        )
    for copy in a2a:
        copy.start()
    pending += a2a

    def forward(i, src):
        block = flip(me, i) * n_chan + chan
        for j in range(1, n_chan):
            copy = remote(
                src,
                ext.at[block],
                fwd_s.at[j - 1, i],
                fwd_r.at[j - 1, i],
                device(me, chan_at(j)),
            )
            copy.start()
            forwards[i].append(copy)

    forwards = [[] for _ in range(owners)]
    brick_blocks = n_sub * n_chan

    def pass_on(m):
        for i in range(m * n_sub, (m + 1) * n_sub):
            if i == 0:
                forward(0, ordered.at[me])
                ext[me * n_chan + chan] = ordered[me]
            else:
                a2a[i - 1].wait_recv()
                forward(i, ext.at[flip(me, i) * n_chan + chan])

    def collect(m):
        for i in range(m * n_sub, (m + 1) * n_sub):
            for copy in forwards[i]:
                copy.wait_recv()

    def multiply(m):
        place = pl.ds(flip(lax.axis_index("brick"), m) * brick_blocks, brick_blocks)
        products(ext[place].reshape(brick_blocks * BLK, channels), conv1_w, prod, place)

    pass_on(0)
    spare = conv1_w.shape[0] - taps * width
    if spare:
        conv1_w[pl.ds(taps * width, spare), :] = jnp.zeros((spare, channels), jnp.bfloat16)
        conv2_w[pl.ds(taps * width, spare), :] = jnp.zeros((spare, channels), jnp.bfloat16)
    for k in range(taps):
        prod[k, blocks + 2 * hcap] = jnp.zeros((BLK, width), jnp.float32)

    for load in staged[2:]:
        load.wait()
    slots = tile_out.shape[2]
    kids = down_w.shape[0]
    cells = BLK // kids
    capacity = slots // cells
    column = lax.broadcasted_iota(jnp.int32, (1, blocks * cells), 1)
    target_row = lax.rem(column, cells)
    names = [down_route[0, n] for n in range(blocks)]
    for n in range(blocks):
        earlier = jnp.int32(0)
        for before in range(n):
            earlier = earlier + jnp.where(names[before] == names[n], 1, 0)
        position = (names[n] * capacity + earlier) * cells
        target_row = target_row + jnp.where(lax.div(column, cells) == n, position, 0)
    slot_row = lax.broadcasted_iota(jnp.int32, (owners * slots, blocks * cells), 0)
    selector[...] = jnp.where(slot_row == target_row, 1.0, 0.0).astype(jnp.bfloat16)
    loads[0].wait()
    for m in range(1, n_brick):
        pass_on(m)
    for m in range(n_brick - 1):
        collect(m)
        multiply(m)
    collect(n_brick - 1)
    pending += [copy for copies in forwards for copy in copies]

    has_next, has_last = me < owners - 1, me > 0

    def halo_copies(direction):
        return remote(
            halo_out.at[direction],
            halo_in.at[direction],
            halo_s.at[direction],
            halo_r.at[direction],
            device(owner_at(1 if direction == 0 else -1), chan),
        )

    for direction, sends in ((0, has_next), (1, has_last)):
        for j in range(hcap):
            halo_out[direction, j] = ext[halo_send[direction, j]]
        pl.when(sends)(lambda direction=direction: halo_copies(direction).start())
    multiply(n_brick - 1)
    for direction, receives in ((0, has_last), (1, has_next)):

        @pl.when(receives)
        def _():
            halo_copies(direction).wait_recv()

        @pl.when(jnp.logical_not(receives))
        def _():
            halo_in[direction] = jnp.zeros((hcap, BLK, channels), jnp.bfloat16)

    rim = pl.ds(blocks, 2 * hcap)
    products(halo_in[...].reshape(2 * hcap * BLK, channels), conv1_w, prod, rim)

    def first_hidden(n):
        scaled = gathered_sum(prod, kernel_map, n) * gain_first[...] + bias_first[...]
        return jnp.maximum(scaled, 0.0).astype(jnp.bfloat16)

    def hid_halo_copies(direction):
        return [
            remote(
                hid_halo_out.at[direction],
                hid_halo_in.at[direction, j],
                hh_s.at[direction, j],
                hh_r.at[direction, j],
                device(owner_at(1 if direction == 0 else -1), chan_at(j)),
            )
            for j in range(n_chan)
        ]

    for direction, sends in ((0, has_next), (1, has_last)):
        for j in range(hcap):
            hid_halo_out[direction, j] = first_hidden(halo_send[direction, j])

        @pl.when(sends)
        def _():
            for copy in hid_halo_copies(direction):
                copy.start()

    hid_copies = []
    for g in range(group_count):

        def first_block(n, carry):
            hid_own[n] = first_hidden(n)
            return carry

        lax.fori_loop(g * group, (g + 1) * group, first_block, 0, unroll=2)
        place = pl.ds(g * group, group)
        for j in range(1, n_chan):
            copy = remote(
                hid_own.at[place],
                hid_in.at[j - 1, place],
                hid_s.at[j - 1, g],
                hid_r.at[j - 1, g],
                device(me, chan_at(j)),
            )
            copy.start()
            hid_copies.append(copy)
    pending += hid_copies

    for load in loads[2:]:
        load.wait()
    def second_products(g):
        place = pl.ds(g * group, group)
        halves = [hid_own[place]]
        for j in range(1, n_chan):
            hid_copies[g * (n_chan - 1) + j - 1].wait_recv()
            halves.append(hid_in[j - 1, place])
        lhs = jnp.concatenate([half.reshape(group * BLK, width) for half in halves], axis=1)
        products(lhs, conv2_w, prod, place)

    for g in range(group_count - 1):
        second_products(g)
    for direction, receives in ((0, has_last), (1, has_next)):

        @pl.when(receives)
        def _():
            for copy in hid_halo_copies(direction):
                copy.wait_recv()

        @pl.when(jnp.logical_not(receives))
        def _():
            hid_halo_in[direction] = jnp.zeros(hid_halo_in.shape[1:], jnp.bfloat16)

    halves = [hid_halo_in[:, j].reshape(2 * hcap * BLK, width) for j in range(n_chan)]
    products(jnp.concatenate(halves, axis=1), conv2_w, prod, rim)
    second_products(group_count - 1)
    loads[1].wait()

    def second_block(n, carry):
        second = gathered_sum(prod, kernel_map, n)
        residual = ext[n, :, own_cols].astype(jnp.float32)
        refined = jnp.maximum(second * gain_second[...] + bias_second[...] + residual, 0.0)
        refined = refined.reshape(kids, cells, width)
        for o in range(kids):
            kids_ref[o, n] = refined[o]
        return carry

    lax.fori_loop(0, blocks, second_block, 0, unroll=4)
    partial = None
    for o in range(0, kids, 2):
        child = jnp.concatenate(
            [kids_ref[o + h].reshape(blocks * cells, width) for h in range(2)], axis=1
        ).astype(jnp.bfloat16)
        weight = down_w[o : o + 2].reshape(2 * width, channels)
        product = jnp.dot(child, weight, preferred_element_type=jnp.float32)
        partial = product if partial is None else partial + product
    mine = [chan == c for c in range(n_chan)]
    scale = jnp.concatenate([jnp.where(own, gain_down[...], 1.0) for own in mine], axis=1)
    shift = jnp.concatenate([jnp.where(own, bias_down[...], 0.0) for own in mine], axis=1)
    sides = (partial * scale + shift).astype(jnp.bfloat16)
    outgoing = jnp.dot(selector[...], sides, preferred_element_type=jnp.float32)
    for c in range(n_chan):
        half = outgoing[:, c * width : (c + 1) * width].astype(jnp.bfloat16)
        tile_out[c] = half.reshape(owners, slots, width)

    def send_tile(c, target):
        side = lax.rem(c - chan + n_chan, n_chan)
        copy = remote(
            tile_out.at[c, target],
            tile_in.at[side, me],
            tile_s.at[side, target],
            tile_r.at[side, me],
            device(target, c),
        )
        pl.when(jnp.logical_or(me != target, chan != c))(copy.start)

    def tiles(act):
        for other in range(owners):
            for side in range(n_chan):
                copy = remote(
                    tile_out.at[side, other],
                    tile_in.at[side, other],
                    tile_s.at[side, other],
                    tile_r.at[side, other],
                    device(other, chan_at(side)),
                )
                if side:
                    act(copy)
                else:
                    pl.when(me != other)(functools.partial(act, copy))

    for c in range(n_chan):
        for target in range(n_sub):
            send_tile(c, target)
    for target in reversed(range(n_sub, owners)):
        for c in range(n_chan):
            send_tile(c, target)
    tile_in[0, me] = tile_out[chan, me]
    for copy in pending:
        copy.wait_send()
    for direction, sends in ((0, has_next), (1, has_last)):

        @pl.when(sends)
        def _():
            halo_copies(direction).wait_send()
            for copy in hid_halo_copies(direction):
                copy.wait_send()

    tiles(lambda copy: copy.wait_recv())
    arrived = tile_in[0].reshape(owners * slots, width).astype(jnp.float32)
    for j in range(1, n_chan):
        other = tile_in[j].reshape(owners * slots, width).astype(jnp.float32)
        arrived = arrived + other * gain_down[...]
    out[0] = jnp.maximum(arrived, 0.0).T.astype(jnp.bfloat16)
    tiles(lambda copy: copy.wait_send())


def fused(axes, features, scan_order, kernel_map, halo_send, down_route, w1, w2, wd, *scales):
    n_brick, n_chan, n_sub = axes
    owners = n_brick * n_sub
    blocks = kernel_map.shape[0]
    channels = features.shape[1]
    width = w1.shape[1]
    hcap = halo_send.shape[1]
    taps = kernel_map.shape[1]
    even_taps = taps + taps % 2
    cells = BLK // wd.shape[0]
    slots = max(2, 2 * blocks // owners) * cells
    groups = 4
    bf16, f32 = jnp.bfloat16, jnp.float32
    vmem = pl.BlockSpec(memory_space=pltpu.VMEM)
    hbm = pl.BlockSpec(memory_space=pl.ANY)

    def pair(*shape):
        return [pltpu.SemaphoreType.DMA(shape), pltpu.SemaphoreType.DMA(shape)]

    return pl.pallas_call(
        functools.partial(fused_kernel, axes),
        out_shape=pltpu.VMEM((1, width, owners * slots), bf16),
        in_specs=[hbm] * 14,
        out_specs=vmem,
        scratch_shapes=[
            pltpu.VMEM(features.shape, bf16),
            pltpu.VMEM(scan_order.shape, jnp.int32),
            pltpu.SMEM(kernel_map.shape, jnp.int32),
            pltpu.SMEM(halo_send.shape, jnp.int32),
            pltpu.SMEM((1, blocks), jnp.int32),
            *[pltpu.VMEM((1, width), f32)] * 6,
            pltpu.SemaphoreType.DMA((11,)),
            pltpu.VMEM((even_taps * width, channels), bf16),
            pltpu.VMEM((even_taps * width, channels), bf16),
            pltpu.VMEM(wd.shape, bf16),
            pltpu.VMEM((owners, BLK, channels), bf16),
            pltpu.VMEM((blocks, BLK, channels), bf16),
            pltpu.VMEM((2, hcap, BLK, channels), bf16),
            pltpu.VMEM((2, hcap, BLK, channels), bf16),
            pltpu.VMEM((blocks, BLK, width), bf16),
            pltpu.VMEM((n_chan - 1, blocks, BLK, width), bf16),
            pltpu.VMEM((2, hcap, BLK, width), bf16),
            pltpu.VMEM((2, n_chan, hcap, BLK, width), bf16),
            pltpu.VMEM((even_taps, blocks + 2 * hcap + 1, BLK, width), f32),
            pltpu.VMEM((wd.shape[0], blocks, cells, width), f32),
            pltpu.VMEM((owners * slots, blocks * cells), bf16),
            pltpu.VMEM((n_chan, owners, slots, width), bf16),
            pltpu.VMEM((n_chan, owners, slots, width), bf16),
            pltpu.SemaphoreType.DMA((2 + n_chan,)),
            *pair(owners - 1),
            *pair(n_chan - 1, owners),
            *pair(2),
            *pair(n_chan - 1, groups),
            *pair(2, n_chan),
            *pair(n_chan, owners),
        ],
        compiler_params=pltpu.CompilerParams(
            collective_id=0, has_side_effects=True, vmem_limit_bytes=66977792
        ),
        name="encoder_level",
    )(
        features,
        scan_order,
        kernel_map,
        halo_send,
        down_route.reshape(1, blocks),
        w1.reshape(taps * width, channels),
        w2.reshape(taps * width, channels),
        wd,
        *[scale.reshape(1, width) for scale in scales],
    )


def fits(axes, features, kernel_map, width):
    n_brick, n_chan, n_sub = axes
    owners = n_brick * n_sub
    whole = width % LANES == 0 and n_chan > 1 and kernel_map.shape[0] % 4 == 0
    whole = whole and owners & (owners - 1) == 0 and n_sub & (n_sub - 1) == 0
    return whole and features.shape[0] == owners * BLK and kernel_map.shape[0] == owners * n_chan


def from_behind(block, axis, distance):
    devices = range(lax.axis_size(axis))
    route = [(i - distance, i) for i in devices if i - distance in devices]
    return lax.ppermute(block, axis, route)


def neighbours(blocks, step_by):
    return from_behind(blocks, ("brick", "sub"), step_by)


def picked(index, source):
    chosen = jnp.arange(source.shape[0], dtype=jnp.int32)[None, :] == index[:, None]
    flat = source.reshape(source.shape[0], -1)
    rows = jnp.dot(chosen.astype(source.dtype), flat, preferred_element_type=jnp.float32)
    return rows.astype(source.dtype).reshape(index.shape[0], *source.shape[1:])


def convolve(extended, weight, kernel_map):
    block_count = kernel_map.shape[0]

    def one_tap(running, inputs):
        tap_weight, index = inputs
        return running + jnp.einsum(
            "brc,dc->brd",
            picked(index, extended),
            tap_weight,
            preferred_element_type=jnp.float32,
        ), None

    initial = jnp.zeros((block_count, BLK, weight.shape[1]), jnp.float32)
    running, _ = lax.scan(one_tap, initial, (weight, kernel_map.T))
    return running


def body(
    features,
    scan_order,
    kernel_map,
    halo_send,
    down_route,
    conv1_weight,
    conv2_weight,
    down_weight,
    gain_first,
    bias_first,
    gain_second,
    bias_second,
    gain_down,
    bias_down,
):
    axes = tuple(lax.axis_size(name) for name in ("brick", "chan", "sub"))
    if fits(axes, features, kernel_map, conv1_weight.shape[1]):
        return fused(
            axes,
            features,
            scan_order,
            kernel_map,
            halo_send,
            down_route,
            conv1_weight,
            conv2_weight,
            down_weight,
            gain_first,
            bias_first,
            gain_second,
            bias_second,
            gain_down,
            bias_down,
        )
    owners = lax.axis_size(("brick", "sub"))
    per_owner = features.shape[0] // owners
    channels = features.shape[1]
    width_out = conv1_weight.shape[1]
    block_count = kernel_map.shape[0]
    channel_start = lax.axis_index("chan") * width_out
    ordered = picked(scan_order[0], features).reshape(owners, per_owner, channels)
    regrouped = lax.all_to_all(ordered, ("brick", "sub"), split_axis=0, concat_axis=0, tiled=True)
    owner_rows = lax.all_gather(regrouped, "chan", axis=1, tiled=True)
    row_blocks = owner_rows.reshape(block_count, BLK, channels)

    def extend(own):
        from_lower = neighbours(picked(halo_send[0], own), 1)
        from_upper = neighbours(picked(halo_send[1], own), -1)
        empty = jnp.zeros((1, BLK, channels), jnp.bfloat16)
        return jnp.concatenate([own, from_lower, from_upper, empty], axis=0)

    conv_first = convolve(extend(row_blocks), conv1_weight, kernel_map)
    hidden = jax.nn.relu(conv_first * gain_first + bias_first).astype(jnp.bfloat16)
    all_channels = lax.all_gather(hidden, "chan", axis=2, tiled=True)
    second = convolve(extend(all_channels), conv2_weight, kernel_map)
    residual = lax.dynamic_slice_in_dim(row_blocks, channel_start, width_out, 2)
    refined = jax.nn.relu(second * gain_second + bias_second + residual.astype(jnp.float32))
    children = refined.astype(jnp.bfloat16).reshape(block_count, 8, 8, width_out)
    partial_value = jnp.einsum(
        "oic,noqi->cnq", down_weight, children, preferred_element_type=jnp.float32
    )
    coarse = lax.psum_scatter(
        partial_value.reshape(width_out * lax.axis_size("chan"), block_count * 8).astype(
            jnp.bfloat16
        ),
        "chan",
        scatter_dimension=0,
        tiled=True,
    ).astype(jnp.float32)
    tile_values = jax.nn.relu(coarse * gain_down[:, None] + bias_down[:, None]).astype(jnp.bfloat16)
    tile_values = tile_values.reshape(width_out, block_count, 8)
    capacity = max(2, 2 * block_count // owners)
    destination = down_route[:, 0]
    number = jnp.arange(block_count, dtype=jnp.int32)
    alike = (destination[:, None] == destination[None, :]) & (number[:, None] > number[None, :])
    position = destination * capacity + jnp.sum(alike.astype(jnp.int32), axis=1)
    selector = (
        position[None, :] == jnp.arange(owners * capacity, dtype=jnp.int32)[:, None]
    ).astype(jnp.bfloat16)
    outgoing = jnp.einsum(
        "pn,cnq->cpq", selector, tile_values, preferred_element_type=jnp.float32
    ).astype(jnp.bfloat16)
    outgoing = outgoing.reshape(width_out, owners, capacity * 8)
    arrived = lax.all_to_all(outgoing, ("brick", "sub"), split_axis=1, concat_axis=2, tiled=True)
    return arrived.reshape(1, width_out, owners * capacity * 8)


def solution(mesh):
    placed = (
        P(("groups", "brick", "chan", "sub"), None),
        P(("groups", "brick", "chan", "sub"), None),
        P(("groups", "brick", "sub"), None),
        P(("groups", "brick", "sub"), None),
        P(("groups", "brick", "sub"), None),
        P(None, "chan", None),
        P(None, "chan", None),
        P(None, "chan", None),
        P("chan"),
        P("chan"),
        P("chan"),
        P("chan"),
        P("chan"),
        P("chan"),
    )
    return jax.shard_map(
        body,
        mesh=mesh,
        in_specs=placed,
        out_specs=P(("groups", "brick", "sub"), "chan", None),
        check_vma=False,
    )
```

```python
import functools

import jax
import jax.numpy as jnp
from jax import lax
from jax.experimental import pallas as pl
from jax.experimental.pallas import tpu as pltpu
from jax.sharding import PartitionSpec as P

BLK = 64
LANES = 128
MESH = pl.DeviceIdType.MESH


def products(lhs, weight, prod, place):
    width = prod.shape[3]
    shape = (lhs.shape[0] // BLK, BLK, width)

    def step(pair, carry):
        both = weight[pl.ds(pl.multiple_of(pair * 2 * width, 2 * width), 2 * width), :]
        result = lax.dot_general(
            lhs, both, (((1,), (1,)), ((), ())), preferred_element_type=jnp.float32
        )
        prod[2 * pair, place] = result[:, :width].reshape(shape)
        prod[2 * pair + 1, place] = result[:, width:].reshape(shape)
        return carry

    lax.fori_loop(0, prod.shape[0] // 2, step, 0, unroll=True)


def gathered_sum(prod, kernel_map, n):
    total = None
    for k in range(kernel_map.shape[1]):
        term = prod[k, kernel_map[n, k]]
        total = term if total is None else total + term
    return total


def flip(x, bits):
    result = x
    weight = 1
    while weight <= bits:
        if bits & weight:
            result = result + weight - 2 * weight * lax.rem(lax.div(x, weight), 2)
        weight *= 2
    return result


def fused_kernel(
    axes,
    features_hbm,
    scan_order_hbm,
    kernel_map_hbm,
    halo_send_hbm,
    down_route_hbm,
    conv1_hbm,
    conv2_hbm,
    down_hbm,
    gain_first_hbm,
    bias_first_hbm,
    gain_second_hbm,
    bias_second_hbm,
    gain_down_hbm,
    bias_down_hbm,
    out,
    features,
    scan_order,
    kernel_map,
    halo_send,
    down_route,
    gain_first,
    bias_first,
    gain_second,
    bias_second,
    gain_down,
    bias_down,
    stage_sem,
    conv1_w,
    conv2_w,
    down_w,
    ordered,
    ext,
    halo_out,
    halo_in,
    hid_own,
    hid_in,
    hid_halo_out,
    hid_halo_in,
    prod,
    kids_ref,
    selector,
    tile_out,
    tile_in,
    w_sem,
    a2a_s,
    a2a_r,
    fwd_s,
    fwd_r,
    halo_s,
    halo_r,
    hid_s,
    hid_r,
    hh_s,
    hh_r,
    tile_s,
    tile_r,
):
    staged = [
        pltpu.make_async_copy(source, place, stage_sem.at[i])
        for i, (source, place) in enumerate(
            [
                (features_hbm, features),
                (scan_order_hbm, scan_order),
                (kernel_map_hbm, kernel_map),
                (halo_send_hbm, halo_send),
                (down_route_hbm, down_route),
                (gain_first_hbm, gain_first),
                (bias_first_hbm, bias_first),
                (gain_second_hbm, gain_second),
                (bias_second_hbm, bias_second),
                (gain_down_hbm, gain_down),
                (bias_down_hbm, bias_down),
            ]
        )
    ]
    for load in staged:
        load.start()
    n_brick, n_chan, n_sub = axes
    owners = n_brick * n_sub
    blocks = kernel_map.shape[0]
    channels = features.shape[1]
    width = out.shape[1]
    hcap = halo_send.shape[1]
    group_count = hid_s.shape[1]
    group = blocks // group_count
    me_group = lax.axis_index("groups")
    chan = lax.axis_index("chan")
    me = lax.axis_index("brick") * n_sub + lax.axis_index("sub")
    own_cols = pl.ds(pl.multiple_of(chan * width, LANES), width)

    def device(owner, c):
        return (me_group, lax.div(owner, n_sub), c, lax.rem(owner, n_sub))

    def owner_at(shift):
        return lax.rem(me + shift + owners, owners)

    def chan_at(shift):
        return lax.rem(chan + shift + n_chan, n_chan)

    def remote(src, dst, send, recv, target):
        return pltpu.make_async_remote_copy(
            src_ref=src,
            dst_ref=dst,
            send_sem=send,
            recv_sem=recv,
            device_id=target,
            device_id_type=MESH,
        )

    taps = kernel_map.shape[1]
    loads = [
        pltpu.make_async_copy(conv1_hbm, conv1_w.at[pl.ds(0, taps * width)], w_sem.at[0]),
        pltpu.make_async_copy(down_hbm, down_w, w_sem.at[1]),
    ]

    def cols_from(j):
        return pl.ds(pl.multiple_of(chan_at(-j) * width, LANES), width)

    for j in range(n_chan):
        target = conv2_w.at[pl.ds(0, taps * width), pl.ds(j * width, width)]
        loads.append(
            pltpu.make_async_copy(conv2_hbm.at[:, cols_from(j)], target, w_sem.at[2 + j])
        )
    barrier = pltpu.get_barrier_semaphore()
    partners = [device(flip(me, i), chan) for i in reversed(range(1, owners))]
    partners += [device(me, chan_at(j)) for j in range(1, n_chan)]
    for partner in partners:
        pl.semaphore_signal(barrier, inc=1, device_id=partner, device_id_type=MESH)
    for load in loads:
        load.start()

    for load in staged[:2]:
        load.wait()
    count = features.shape[0]
    source_row = lax.broadcasted_iota(jnp.int32, (count, count), 0)
    chosen = jnp.where(source_row == scan_order[...], 1.0, 0.0).astype(jnp.bfloat16)
    rows = lax.dot_general(
        chosen, features[...], (((0,), (0,)), ((), ())), preferred_element_type=jnp.float32
    ).astype(jnp.bfloat16)
    ordered[...] = rows.reshape(owners, BLK, channels)

    pl.semaphore_wait(barrier, len(partners))

    pending = []
    a2a = []
    for i in range(1, owners):
        target = flip(me, i)
        a2a.append(
            remote(
                ordered.at[target],
                ext.at[me * n_chan + chan],
                a2a_s.at[i - 1],
                a2a_r.at[i - 1],
                device(target, chan),
            )
        )
    for copy in a2a:
        copy.start()
    pending += a2a

    def forward(i, src):
        block = flip(me, i) * n_chan + chan
        for j in range(1, n_chan):
            copy = remote(
                src,
                ext.at[block],
                fwd_s.at[j - 1, i],
                fwd_r.at[j - 1, i],
                device(me, chan_at(j)),
            )
            copy.start()
            forwards[i].append(copy)

    forwards = [[] for _ in range(owners)]
    brick_blocks = n_sub * n_chan

    def pass_on(m):
        for i in range(m * n_sub, (m + 1) * n_sub):
            if i == 0:
                forward(0, ordered.at[me])
                ext[me * n_chan + chan] = ordered[me]
            else:
                a2a[i - 1].wait_recv()
                forward(i, ext.at[flip(me, i) * n_chan + chan])

    def collect(m):
        for i in range(m * n_sub, (m + 1) * n_sub):
            for copy in forwards[i]:
                copy.wait_recv()

    def multiply(m):
        place = pl.ds(flip(lax.axis_index("brick"), m) * brick_blocks, brick_blocks)
        products(ext[place].reshape(brick_blocks * BLK, channels), conv1_w, prod, place)

    pass_on(0)
    spare = conv1_w.shape[0] - taps * width
    if spare:
        conv1_w[pl.ds(taps * width, spare), :] = jnp.zeros((spare, channels), jnp.bfloat16)
        conv2_w[pl.ds(taps * width, spare), :] = jnp.zeros((spare, channels), jnp.bfloat16)
    for k in range(taps):
        prod[k, blocks + 2 * hcap] = jnp.zeros((BLK, width), jnp.float32)

    for load in staged[2:]:
        load.wait()
    slots = tile_out.shape[2]
    kids = down_w.shape[0]
    cells = BLK // kids
    capacity = slots // cells
    column = lax.broadcasted_iota(jnp.int32, (1, blocks * cells), 1)
    target_row = lax.rem(column, cells)
    names = [down_route[0, n] for n in range(blocks)]
    for n in range(blocks):
        earlier = jnp.int32(0)
        for before in range(n):
            earlier = earlier + jnp.where(names[before] == names[n], 1, 0)
        position = (names[n] * capacity + earlier) * cells
        target_row = target_row + jnp.where(lax.div(column, cells) == n, position, 0)
    slot_row = lax.broadcasted_iota(jnp.int32, (owners * slots, blocks * cells), 0)
    selector[...] = jnp.where(slot_row == target_row, 1.0, 0.0).astype(jnp.bfloat16)
    loads[0].wait()
    for m in range(1, n_brick):
        pass_on(m)
    for m in range(n_brick - 1):
        collect(m)
        multiply(m)
    collect(n_brick - 1)
    pending += [copy for copies in forwards for copy in copies]

    has_next, has_last = me < owners - 1, me > 0

    def halo_copies(direction):
        return remote(
            halo_out.at[direction],
            halo_in.at[direction],
            halo_s.at[direction],
            halo_r.at[direction],
            device(owner_at(1 if direction == 0 else -1), chan),
        )

    for direction, sends in ((1, has_last), (0, has_next)):
        for j in range(hcap):
            halo_out[direction, j] = ext[halo_send[direction, j]]
        pl.when(sends)(lambda direction=direction: halo_copies(direction).start())
    multiply(n_brick - 1)
    for direction, receives in ((0, has_last), (1, has_next)):

        @pl.when(receives)
        def _():
            halo_copies(direction).wait_recv()

        @pl.when(jnp.logical_not(receives))
        def _():
            halo_in[direction] = jnp.zeros((hcap, BLK, channels), jnp.bfloat16)

    rim = pl.ds(blocks, 2 * hcap)
    products(halo_in[...].reshape(2 * hcap * BLK, channels), conv1_w, prod, rim)

    def first_hidden(n):
        scaled = gathered_sum(prod, kernel_map, n) * gain_first[...] + bias_first[...]
        return jnp.maximum(scaled, 0.0).astype(jnp.bfloat16)

    def hid_halo_copies(direction):
        return [
            remote(
                hid_halo_out.at[direction],
                hid_halo_in.at[direction, j],
                hh_s.at[direction, j],
                hh_r.at[direction, j],
                device(owner_at(1 if direction == 0 else -1), chan_at(j)),
            )
            for j in range(n_chan)
        ]

    for direction, sends in ((1, has_last), (0, has_next)):
        for j in range(hcap):
            hid_halo_out[direction, j] = first_hidden(halo_send[direction, j])

        @pl.when(sends)
        def _():
            for copy in hid_halo_copies(direction):
                copy.start()

    hid_copies = []
    for g in range(group_count):

        def first_block(n, carry):
            hid_own[n] = first_hidden(n)
            return carry

        lax.fori_loop(g * group, (g + 1) * group, first_block, 0, unroll=2)
        place = pl.ds(g * group, group)
        for j in range(1, n_chan):
            copy = remote(
                hid_own.at[place],
                hid_in.at[j - 1, place],
                hid_s.at[j - 1, g],
                hid_r.at[j - 1, g],
                device(me, chan_at(j)),
            )
            copy.start()
            hid_copies.append(copy)
    pending += hid_copies

    for load in loads[2:]:
        load.wait()
    def second_products(g):
        place = pl.ds(g * group, group)
        halves = [hid_own[place]]
        for j in range(1, n_chan):
            hid_copies[g * (n_chan - 1) + j - 1].wait_recv()
            halves.append(hid_in[j - 1, place])
        lhs = jnp.concatenate([half.reshape(group * BLK, width) for half in halves], axis=1)
        products(lhs, conv2_w, prod, place)

    for g in range(group_count - 1):
        second_products(g)
    for direction, receives in ((0, has_last), (1, has_next)):

        @pl.when(receives)
        def _():
            for copy in hid_halo_copies(direction):
                copy.wait_recv()

        @pl.when(jnp.logical_not(receives))
        def _():
            hid_halo_in[direction] = jnp.zeros(hid_halo_in.shape[1:], jnp.bfloat16)

    halves = [hid_halo_in[:, j].reshape(2 * hcap * BLK, width) for j in range(n_chan)]
    products(jnp.concatenate(halves, axis=1), conv2_w, prod, rim)
    second_products(group_count - 1)
    loads[1].wait()

    def second_block(n, carry):
        second = gathered_sum(prod, kernel_map, n)
        residual = ext[n, :, own_cols].astype(jnp.float32)
        refined = jnp.maximum(second * gain_second[...] + bias_second[...] + residual, 0.0)
        refined = refined.reshape(kids, cells, width)
        for o in range(kids):
            kids_ref[o, n] = refined[o]
        return carry

    lax.fori_loop(0, blocks, second_block, 0, unroll=4)
    partial = None
    for o in range(0, kids, 2):
        child = jnp.concatenate(
            [kids_ref[o + h].reshape(blocks * cells, width) for h in range(2)], axis=1
        ).astype(jnp.bfloat16)
        weight = down_w[o : o + 2].reshape(2 * width, channels)
        product = jnp.dot(child, weight, preferred_element_type=jnp.float32)
        partial = product if partial is None else partial + product
    mine = [chan == c for c in range(n_chan)]
    scale = jnp.concatenate([jnp.where(own, gain_down[...], 1.0) for own in mine], axis=1)
    shift = jnp.concatenate([jnp.where(own, bias_down[...], 0.0) for own in mine], axis=1)
    sides = (partial * scale + shift).astype(jnp.bfloat16)
    def pack_tiles(first, last):
        chosen = selector[first * slots : last * slots, :]
        outgoing = jnp.dot(chosen, sides, preferred_element_type=jnp.float32)
        for c in range(n_chan):
            half = outgoing[:, c * width : (c + 1) * width].astype(jnp.bfloat16)
            tile_out[c, first:last] = half.reshape(last - first, slots, width)

    def send_tile(c, target):
        side = lax.rem(c - chan + n_chan, n_chan)
        copy = remote(
            tile_out.at[c, target],
            tile_in.at[side, me],
            tile_s.at[side, target],
            tile_r.at[side, me],
            device(target, c),
        )
        pl.when(jnp.logical_or(me != target, chan != c))(copy.start)

    def tiles(act):
        for other in range(owners):
            for side in range(n_chan):
                copy = remote(
                    tile_out.at[side, other],
                    tile_in.at[side, other],
                    tile_s.at[side, other],
                    tile_r.at[side, other],
                    device(other, chan_at(side)),
                )
                if side:
                    act(copy)
                else:
                    pl.when(me != other)(functools.partial(act, copy))

    pack_tiles(0, n_sub)
    for c in range(n_chan):
        for target in range(n_sub):
            send_tile(c, target)
    pack_tiles(n_sub, owners)
    for target in reversed(range(n_sub, owners)):
        for c in range(n_chan):
            send_tile(c, target)
    tile_in[0, me] = tile_out[chan, me]
    for copy in pending:
        copy.wait_send()
    for direction, sends in ((0, has_next), (1, has_last)):

        @pl.when(sends)
        def _():
            halo_copies(direction).wait_send()
            for copy in hid_halo_copies(direction):
                copy.wait_send()

    tiles(lambda copy: copy.wait_recv())
    arrived = tile_in[0].reshape(owners * slots, width).astype(jnp.float32)
    for j in range(1, n_chan):
        other = tile_in[j].reshape(owners * slots, width).astype(jnp.float32)
        arrived = arrived + other * gain_down[...]
    out[0] = jnp.maximum(arrived, 0.0).T.astype(jnp.bfloat16)
    tiles(lambda copy: copy.wait_send())


def fused(axes, features, scan_order, kernel_map, halo_send, down_route, w1, w2, wd, *scales):
    n_brick, n_chan, n_sub = axes
    owners = n_brick * n_sub
    blocks = kernel_map.shape[0]
    channels = features.shape[1]
    width = w1.shape[1]
    hcap = halo_send.shape[1]
    taps = kernel_map.shape[1]
    even_taps = taps + taps % 2
    cells = BLK // wd.shape[0]
    slots = max(2, 2 * blocks // owners) * cells
    groups = 4
    bf16, f32 = jnp.bfloat16, jnp.float32
    vmem = pl.BlockSpec(memory_space=pltpu.VMEM)
    hbm = pl.BlockSpec(memory_space=pl.ANY)

    def pair(*shape):
        return [pltpu.SemaphoreType.DMA(shape), pltpu.SemaphoreType.DMA(shape)]

    return pl.pallas_call(
        functools.partial(fused_kernel, axes),
        out_shape=pltpu.VMEM((1, width, owners * slots), bf16),
        in_specs=[hbm] * 14,
        out_specs=vmem,
        scratch_shapes=[
            pltpu.VMEM(features.shape, bf16),
            pltpu.VMEM(scan_order.shape, jnp.int32),
            pltpu.SMEM(kernel_map.shape, jnp.int32),
            pltpu.SMEM(halo_send.shape, jnp.int32),
            pltpu.SMEM((1, blocks), jnp.int32),
            *[pltpu.VMEM((1, width), f32)] * 6,
            pltpu.SemaphoreType.DMA((11,)),
            pltpu.VMEM((even_taps * width, channels), bf16),
            pltpu.VMEM((even_taps * width, channels), bf16),
            pltpu.VMEM(wd.shape, bf16),
            pltpu.VMEM((owners, BLK, channels), bf16),
            pltpu.VMEM((blocks, BLK, channels), bf16),
            pltpu.VMEM((2, hcap, BLK, channels), bf16),
            pltpu.VMEM((2, hcap, BLK, channels), bf16),
            pltpu.VMEM((blocks, BLK, width), bf16),
            pltpu.VMEM((n_chan - 1, blocks, BLK, width), bf16),
            pltpu.VMEM((2, hcap, BLK, width), bf16),
            pltpu.VMEM((2, n_chan, hcap, BLK, width), bf16),
            pltpu.VMEM((even_taps, blocks + 2 * hcap + 1, BLK, width), f32),
            pltpu.VMEM((wd.shape[0], blocks, cells, width), f32),
            pltpu.VMEM((owners * slots, blocks * cells), bf16),
            pltpu.VMEM((n_chan, owners, slots, width), bf16),
            pltpu.VMEM((n_chan, owners, slots, width), bf16),
            pltpu.SemaphoreType.DMA((2 + n_chan,)),
            *pair(owners - 1),
            *pair(n_chan - 1, owners),
            *pair(2),
            *pair(n_chan - 1, groups),
            *pair(2, n_chan),
            *pair(n_chan, owners),
        ],
        compiler_params=pltpu.CompilerParams(
            collective_id=0, has_side_effects=True, vmem_limit_bytes=66977792
        ),
        name="encoder_level",
    )(
        features,
        scan_order,
        kernel_map,
        halo_send,
        down_route.reshape(1, blocks),
        w1.reshape(taps * width, channels),
        w2.reshape(taps * width, channels),
        wd,
        *[scale.reshape(1, width) for scale in scales],
    )


def fits(axes, features, kernel_map, width):
    n_brick, n_chan, n_sub = axes
    owners = n_brick * n_sub
    whole = width % LANES == 0 and n_chan > 1 and kernel_map.shape[0] % 4 == 0
    whole = whole and owners & (owners - 1) == 0 and n_sub & (n_sub - 1) == 0
    return whole and features.shape[0] == owners * BLK and kernel_map.shape[0] == owners * n_chan


def from_behind(block, axis, distance):
    devices = range(lax.axis_size(axis))
    route = [(i - distance, i) for i in devices if i - distance in devices]
    return lax.ppermute(block, axis, route)


def neighbours(blocks, step_by):
    return from_behind(blocks, ("brick", "sub"), step_by)


def picked(index, source):
    chosen = jnp.arange(source.shape[0], dtype=jnp.int32)[None, :] == index[:, None]
    flat = source.reshape(source.shape[0], -1)
    rows = jnp.dot(chosen.astype(source.dtype), flat, preferred_element_type=jnp.float32)
    return rows.astype(source.dtype).reshape(index.shape[0], *source.shape[1:])


def convolve(extended, weight, kernel_map):
    block_count = kernel_map.shape[0]

    def one_tap(running, inputs):
        tap_weight, index = inputs
        return running + jnp.einsum(
            "brc,dc->brd",
            picked(index, extended),
            tap_weight,
            preferred_element_type=jnp.float32,
        ), None

    initial = jnp.zeros((block_count, BLK, weight.shape[1]), jnp.float32)
    running, _ = lax.scan(one_tap, initial, (weight, kernel_map.T))
    return running


def body(
    features,
    scan_order,
    kernel_map,
    halo_send,
    down_route,
    conv1_weight,
    conv2_weight,
    down_weight,
    gain_first,
    bias_first,
    gain_second,
    bias_second,
    gain_down,
    bias_down,
):
    axes = tuple(lax.axis_size(name) for name in ("brick", "chan", "sub"))
    if fits(axes, features, kernel_map, conv1_weight.shape[1]):
        return fused(
            axes,
            features,
            scan_order,
            kernel_map,
            halo_send,
            down_route,
            conv1_weight,
            conv2_weight,
            down_weight,
            gain_first,
            bias_first,
            gain_second,
            bias_second,
            gain_down,
            bias_down,
        )
    owners = lax.axis_size(("brick", "sub"))
    per_owner = features.shape[0] // owners
    channels = features.shape[1]
    width_out = conv1_weight.shape[1]
    block_count = kernel_map.shape[0]
    channel_start = lax.axis_index("chan") * width_out
    ordered = picked(scan_order[0], features).reshape(owners, per_owner, channels)
    regrouped = lax.all_to_all(ordered, ("brick", "sub"), split_axis=0, concat_axis=0, tiled=True)
    owner_rows = lax.all_gather(regrouped, "chan", axis=1, tiled=True)
    row_blocks = owner_rows.reshape(block_count, BLK, channels)

    def extend(own):
        from_lower = neighbours(picked(halo_send[0], own), 1)
        from_upper = neighbours(picked(halo_send[1], own), -1)
        empty = jnp.zeros((1, BLK, channels), jnp.bfloat16)
        return jnp.concatenate([own, from_lower, from_upper, empty], axis=0)

    conv_first = convolve(extend(row_blocks), conv1_weight, kernel_map)
    hidden = jax.nn.relu(conv_first * gain_first + bias_first).astype(jnp.bfloat16)
    all_channels = lax.all_gather(hidden, "chan", axis=2, tiled=True)
    second = convolve(extend(all_channels), conv2_weight, kernel_map)
    residual = lax.dynamic_slice_in_dim(row_blocks, channel_start, width_out, 2)
    refined = jax.nn.relu(second * gain_second + bias_second + residual.astype(jnp.float32))
    children = refined.astype(jnp.bfloat16).reshape(block_count, 8, 8, width_out)
    partial_value = jnp.einsum(
        "oic,noqi->cnq", down_weight, children, preferred_element_type=jnp.float32
    )
    coarse = lax.psum_scatter(
        partial_value.reshape(width_out * lax.axis_size("chan"), block_count * 8).astype(
            jnp.bfloat16
        ),
        "chan",
        scatter_dimension=0,
        tiled=True,
    ).astype(jnp.float32)
    tile_values = jax.nn.relu(coarse * gain_down[:, None] + bias_down[:, None]).astype(jnp.bfloat16)
    tile_values = tile_values.reshape(width_out, block_count, 8)
    capacity = max(2, 2 * block_count // owners)
    destination = down_route[:, 0]
    number = jnp.arange(block_count, dtype=jnp.int32)
    alike = (destination[:, None] == destination[None, :]) & (number[:, None] > number[None, :])
    position = destination * capacity + jnp.sum(alike.astype(jnp.int32), axis=1)
    selector = (
        position[None, :] == jnp.arange(owners * capacity, dtype=jnp.int32)[:, None]
    ).astype(jnp.bfloat16)
    outgoing = jnp.einsum(
        "pn,cnq->cpq", selector, tile_values, preferred_element_type=jnp.float32
    ).astype(jnp.bfloat16)
    outgoing = outgoing.reshape(width_out, owners, capacity * 8)
    arrived = lax.all_to_all(outgoing, ("brick", "sub"), split_axis=1, concat_axis=2, tiled=True)
    return arrived.reshape(1, width_out, owners * capacity * 8)


def solution(mesh):
    placed = (
        P(("groups", "brick", "chan", "sub"), None),
        P(("groups", "brick", "chan", "sub"), None),
        P(("groups", "brick", "sub"), None),
        P(("groups", "brick", "sub"), None),
        P(("groups", "brick", "sub"), None),
        P(None, "chan", None),
        P(None, "chan", None),
        P(None, "chan", None),
        P("chan"),
        P("chan"),
        P("chan"),
        P("chan"),
        P("chan"),
        P("chan"),
    )
    return jax.shard_map(
        body,
        mesh=mesh,
        in_specs=placed,
        out_specs=P(("groups", "brick", "sub"), "chan", None),
        check_vma=False,
    )
```

```python
import functools

import jax
import jax.numpy as jnp
from jax import lax
from jax.experimental import pallas as pl
from jax.experimental.pallas import tpu as pltpu
from jax.sharding import PartitionSpec as P

BLK = 64
LANES = 128
MESH = pl.DeviceIdType.MESH


def products(lhs, weight, prod, place):
    width = prod.shape[3]
    shape = (lhs.shape[0] // BLK, BLK, width)

    def step(pair, carry):
        both = weight[pl.ds(pl.multiple_of(pair * 2 * width, 2 * width), 2 * width), :]
        result = lax.dot_general(
            lhs, both, (((1,), (1,)), ((), ())), preferred_element_type=jnp.float32
        )
        prod[2 * pair, place] = result[:, :width].reshape(shape)
        prod[2 * pair + 1, place] = result[:, width:].reshape(shape)
        return carry

    lax.fori_loop(0, prod.shape[0] // 2, step, 0, unroll=True)


def gathered_sum(prod, kernel_map, n):
    total = None
    for k in range(kernel_map.shape[1]):
        term = prod[k, kernel_map[n, k]]
        total = term if total is None else total + term
    return total


def flip(x, bits):
    result = x
    weight = 1
    while weight <= bits:
        if bits & weight:
            result = result + weight - 2 * weight * lax.rem(lax.div(x, weight), 2)
        weight *= 2
    return result


def fused_kernel(
    axes,
    features_hbm,
    scan_order_hbm,
    kernel_map_hbm,
    halo_send_hbm,
    down_route_hbm,
    conv1_hbm,
    conv2_hbm,
    down_hbm,
    gain_first_hbm,
    bias_first_hbm,
    gain_second_hbm,
    bias_second_hbm,
    gain_down_hbm,
    bias_down_hbm,
    out,
    features,
    scan_order,
    kernel_map,
    halo_send,
    down_route,
    gain_first,
    bias_first,
    gain_second,
    bias_second,
    gain_down,
    bias_down,
    stage_sem,
    conv1_w,
    conv2_w,
    down_w,
    ordered,
    ext,
    halo_out,
    halo_in,
    hid_own,
    hid_in,
    hid_halo_out,
    hid_halo_in,
    prod,
    kids_ref,
    selector,
    tile_out,
    tile_in,
    w_sem,
    a2a_s,
    a2a_r,
    fwd_s,
    fwd_r,
    halo_s,
    halo_r,
    hid_s,
    hid_r,
    hh_s,
    hh_r,
    tile_s,
    tile_r,
):
    staged = [
        pltpu.make_async_copy(source, place, stage_sem.at[i])
        for i, (source, place) in enumerate(
            [
                (features_hbm, features),
                (scan_order_hbm, scan_order),
                (kernel_map_hbm, kernel_map),
                (halo_send_hbm, halo_send),
                (down_route_hbm, down_route),
                (gain_first_hbm, gain_first),
                (bias_first_hbm, bias_first),
                (gain_second_hbm, gain_second),
                (bias_second_hbm, bias_second),
                (gain_down_hbm, gain_down),
                (bias_down_hbm, bias_down),
            ]
        )
    ]
    for load in staged:
        load.start()
    n_brick, n_chan, n_sub = axes
    owners = n_brick * n_sub
    blocks = kernel_map.shape[0]
    channels = features.shape[1]
    width = out.shape[1]
    hcap = halo_send.shape[1]
    group_count = hid_s.shape[1]
    group = blocks // group_count
    me_group = lax.axis_index("groups")
    chan = lax.axis_index("chan")
    me = lax.axis_index("brick") * n_sub + lax.axis_index("sub")
    own_cols = pl.ds(pl.multiple_of(chan * width, LANES), width)

    def device(owner, c):
        return (me_group, lax.div(owner, n_sub), c, lax.rem(owner, n_sub))

    def owner_at(shift):
        return lax.rem(me + shift + owners, owners)

    def chan_at(shift):
        return lax.rem(chan + shift + n_chan, n_chan)

    def remote(src, dst, send, recv, target):
        return pltpu.make_async_remote_copy(
            src_ref=src,
            dst_ref=dst,
            send_sem=send,
            recv_sem=recv,
            device_id=target,
            device_id_type=MESH,
        )

    taps = kernel_map.shape[1]
    loads = [
        pltpu.make_async_copy(conv1_hbm, conv1_w.at[pl.ds(0, taps * width)], w_sem.at[0]),
        pltpu.make_async_copy(down_hbm, down_w, w_sem.at[1]),
    ]

    def cols_from(j):
        return pl.ds(pl.multiple_of(chan_at(-j) * width, LANES), width)

    for j in range(n_chan):
        target = conv2_w.at[pl.ds(0, taps * width), pl.ds(j * width, width)]
        loads.append(
            pltpu.make_async_copy(conv2_hbm.at[:, cols_from(j)], target, w_sem.at[2 + j])
        )
    barrier = pltpu.get_barrier_semaphore()
    partners = [device(flip(me, i), chan) for i in reversed(range(1, owners))]
    partners += [device(me, chan_at(j)) for j in range(1, n_chan)]
    for partner in partners:
        pl.semaphore_signal(barrier, inc=1, device_id=partner, device_id_type=MESH)
    for load in loads:
        load.start()

    for load in staged[:2]:
        load.wait()
    count = features.shape[0]
    source_row = lax.broadcasted_iota(jnp.int32, (count, count), 0)
    chosen = jnp.where(source_row == scan_order[...], 1.0, 0.0).astype(jnp.bfloat16)
    rows = lax.dot_general(
        chosen, features[...], (((0,), (0,)), ((), ())), preferred_element_type=jnp.float32
    ).astype(jnp.bfloat16)
    ordered[...] = rows.reshape(owners, BLK, channels)

    pl.semaphore_wait(barrier, len(partners))

    pending = []
    a2a = []
    for i in range(1, owners):
        target = flip(me, i)
        a2a.append(
            remote(
                ordered.at[target],
                ext.at[me * n_chan + chan],
                a2a_s.at[i - 1],
                a2a_r.at[i - 1],
                device(target, chan),
            )
        )
    for copy in a2a:
        copy.start()
    pending += a2a

    def forward(i, src):
        block = flip(me, i) * n_chan + chan
        for j in range(1, n_chan):
            copy = remote(
                src,
                ext.at[block],
                fwd_s.at[j - 1, i],
                fwd_r.at[j - 1, i],
                device(me, chan_at(j)),
            )
            copy.start()
            forwards[i].append(copy)

    forwards = [[] for _ in range(owners)]
    brick_blocks = n_sub * n_chan

    def pass_on(m):
        for i in range(m * n_sub, (m + 1) * n_sub):
            if i == 0:
                forward(0, ordered.at[me])
                ext[me * n_chan + chan] = ordered[me]
            else:
                a2a[i - 1].wait_recv()
                forward(i, ext.at[flip(me, i) * n_chan + chan])

    def collect(m):
        for i in range(m * n_sub, (m + 1) * n_sub):
            for copy in forwards[i]:
                copy.wait_recv()

    def multiply(m):
        place = pl.ds(flip(lax.axis_index("brick"), m) * brick_blocks, brick_blocks)
        products(ext[place].reshape(brick_blocks * BLK, channels), conv1_w, prod, place)

    pass_on(0)
    spare = conv1_w.shape[0] - taps * width
    if spare:
        conv1_w[pl.ds(taps * width, spare), :] = jnp.zeros((spare, channels), jnp.bfloat16)
        conv2_w[pl.ds(taps * width, spare), :] = jnp.zeros((spare, channels), jnp.bfloat16)
    for k in range(taps):
        prod[k, blocks + 2 * hcap] = jnp.zeros((BLK, width), jnp.float32)

    for load in staged[2:]:
        load.wait()
    slots = tile_out.shape[2]
    kids = down_w.shape[0]
    cells = BLK // kids
    capacity = slots // cells
    column = lax.broadcasted_iota(jnp.int32, (1, blocks * cells), 1)
    target_row = lax.rem(column, cells)
    names = [down_route[0, n] for n in range(blocks)]
    for n in range(blocks):
        earlier = jnp.int32(0)
        for before in range(n):
            earlier = earlier + jnp.where(names[before] == names[n], 1, 0)
        position = (names[n] * capacity + earlier) * cells
        target_row = target_row + jnp.where(lax.div(column, cells) == n, position, 0)
    slot_row = lax.broadcasted_iota(jnp.int32, (owners * slots, blocks * cells), 0)
    selector[...] = jnp.where(slot_row == target_row, 1.0, 0.0).astype(jnp.bfloat16)
    loads[0].wait()
    for m in range(1, n_brick):
        pass_on(m)
    for m in range(n_brick - 1):
        collect(m)
        multiply(m)
    collect(n_brick - 1)
    pending += [copy for copies in forwards for copy in copies]

    has_next, has_last = me < owners - 1, me > 0

    def halo_copies(direction):
        return remote(
            halo_out.at[direction],
            halo_in.at[direction],
            halo_s.at[direction],
            halo_r.at[direction],
            device(owner_at(1 if direction == 0 else -1), chan),
        )

    for direction, sends in ((1, has_last), (0, has_next)):
        for j in range(hcap):
            halo_out[direction, j] = ext[halo_send[direction, j]]
        pl.when(sends)(lambda direction=direction: halo_copies(direction).start())
    multiply(n_brick - 1)
    for direction, receives in ((0, has_last), (1, has_next)):

        @pl.when(receives)
        def _():
            halo_copies(direction).wait_recv()

        @pl.when(jnp.logical_not(receives))
        def _():
            halo_in[direction] = jnp.zeros((hcap, BLK, channels), jnp.bfloat16)

    rim = pl.ds(blocks, 2 * hcap)
    products(halo_in[...].reshape(2 * hcap * BLK, channels), conv1_w, prod, rim)

    def first_hidden(n):
        scaled = gathered_sum(prod, kernel_map, n) * gain_first[...] + bias_first[...]
        return jnp.maximum(scaled, 0.0).astype(jnp.bfloat16)

    def hid_halo_copies(direction):
        return [
            remote(
                hid_halo_out.at[direction],
                hid_halo_in.at[direction, j],
                hh_s.at[direction, j],
                hh_r.at[direction, j],
                device(owner_at(1 if direction == 0 else -1), chan_at(j)),
            )
            for j in range(n_chan)
        ]

    for direction, sends in ((1, has_last), (0, has_next)):
        for j in range(hcap):
            hid_halo_out[direction, j] = first_hidden(halo_send[direction, j])

        @pl.when(sends)
        def _():
            for copy in hid_halo_copies(direction):
                copy.start()

    hid_copies = []
    for g in range(group_count):

        def first_block(n, carry):
            hid_own[n] = first_hidden(n)
            return carry

        lax.fori_loop(g * group, (g + 1) * group, first_block, 0, unroll=2)
        place = pl.ds(g * group, group)
        for j in range(1, n_chan):
            copy = remote(
                hid_own.at[place],
                hid_in.at[j - 1, place],
                hid_s.at[j - 1, g],
                hid_r.at[j - 1, g],
                device(me, chan_at(j)),
            )
            copy.start()
            hid_copies.append(copy)
    pending += hid_copies

    for load in loads[2:]:
        load.wait()
    def second_products(g):
        place = pl.ds(g * group, group)
        halves = [hid_own[place]]
        for j in range(1, n_chan):
            hid_copies[g * (n_chan - 1) + j - 1].wait_recv()
            halves.append(hid_in[j - 1, place])
        lhs = jnp.concatenate([half.reshape(group * BLK, width) for half in halves], axis=1)
        products(lhs, conv2_w, prod, place)

    for g in range(group_count - 1):
        second_products(g)
    for direction, receives in ((0, has_last), (1, has_next)):

        @pl.when(receives)
        def _():
            for copy in hid_halo_copies(direction):
                copy.wait_recv()

        @pl.when(jnp.logical_not(receives))
        def _():
            hid_halo_in[direction] = jnp.zeros(hid_halo_in.shape[1:], jnp.bfloat16)

    halves = [hid_halo_in[:, j].reshape(2 * hcap * BLK, width) for j in range(n_chan)]
    products(jnp.concatenate(halves, axis=1), conv2_w, prod, rim)
    second_products(group_count - 1)
    loads[1].wait()

    def second_block(n, carry):
        second = gathered_sum(prod, kernel_map, n)
        residual = ext[n, :, own_cols].astype(jnp.float32)
        refined = jnp.maximum(second * gain_second[...] + bias_second[...] + residual, 0.0)
        refined = refined.reshape(kids, cells, width)
        for o in range(kids):
            kids_ref[o, n] = refined[o]
        return carry

    lax.fori_loop(0, blocks, second_block, 0, unroll=8)
    partial = None
    for o in range(0, kids, 2):
        child = jnp.concatenate(
            [kids_ref[o + h].reshape(blocks * cells, width) for h in range(2)], axis=1
        ).astype(jnp.bfloat16)
        weight = down_w[o : o + 2].reshape(2 * width, channels)
        product = jnp.dot(child, weight, preferred_element_type=jnp.float32)
        partial = product if partial is None else partial + product
    mine = [chan == c for c in range(n_chan)]
    scale = jnp.concatenate([jnp.where(own, gain_down[...], 1.0) for own in mine], axis=1)
    shift = jnp.concatenate([jnp.where(own, bias_down[...], 0.0) for own in mine], axis=1)
    sides = (partial * scale + shift).astype(jnp.bfloat16)
    def pack_tiles(first, last):
        chosen = selector[first * slots : last * slots, :]
        outgoing = jnp.dot(chosen, sides, preferred_element_type=jnp.float32)
        for c in range(n_chan):
            half = outgoing[:, c * width : (c + 1) * width].astype(jnp.bfloat16)
            tile_out[c, first:last] = half.reshape(last - first, slots, width)

    def send_tile(c, target):
        side = lax.rem(c - chan + n_chan, n_chan)
        copy = remote(
            tile_out.at[c, target],
            tile_in.at[side, me],
            tile_s.at[side, target],
            tile_r.at[side, me],
            device(target, c),
        )
        pl.when(jnp.logical_or(me != target, chan != c))(copy.start)

    def tiles(act, others):
        for other in others:
            for side in range(n_chan):
                copy = remote(
                    tile_out.at[side, other],
                    tile_in.at[side, other],
                    tile_s.at[side, other],
                    tile_r.at[side, other],
                    device(other, chan_at(side)),
                )
                if side:
                    act(copy)
                else:
                    pl.when(me != other)(functools.partial(act, copy))

    pack_tiles(0, n_sub)
    for c in range(n_chan):
        for target in range(n_sub):
            send_tile(c, target)
    pack_tiles(n_sub, owners)
    for target in reversed(range(n_sub, owners)):
        for c in range(n_chan):
            send_tile(c, target)
    tile_in[0, me] = tile_out[chan, me]
    for copy in pending:
        copy.wait_send()
    for direction, sends in ((0, has_next), (1, has_last)):

        @pl.when(sends)
        def _():
            halo_copies(direction).wait_send()
            for copy in hid_halo_copies(direction):
                copy.wait_send()

    together = max(1, LANES // slots)
    for first in range(0, owners, together):
        sources = range(first, min(first + together, owners))
        tiles(lambda copy: copy.wait_recv(), sources)
        group = pl.ds(first, len(sources))
        arrived = tile_in[0, group].reshape(len(sources) * slots, width).astype(jnp.float32)
        for j in range(1, n_chan):
            other = tile_in[j, group].reshape(len(sources) * slots, width).astype(jnp.float32)
            arrived = arrived + other * gain_down[...]
        columns = pl.ds(first * slots, len(sources) * slots)
        out[0, :, columns] = jnp.maximum(arrived, 0.0).T.astype(jnp.bfloat16)
    tiles(lambda copy: copy.wait_send(), range(owners))


def fused(axes, features, scan_order, kernel_map, halo_send, down_route, w1, w2, wd, *scales):
    n_brick, n_chan, n_sub = axes
    owners = n_brick * n_sub
    blocks = kernel_map.shape[0]
    channels = features.shape[1]
    width = w1.shape[1]
    hcap = halo_send.shape[1]
    taps = kernel_map.shape[1]
    even_taps = taps + taps % 2
    cells = BLK // wd.shape[0]
    slots = max(2, 2 * blocks // owners) * cells
    groups = 4
    bf16, f32 = jnp.bfloat16, jnp.float32
    vmem = pl.BlockSpec(memory_space=pltpu.VMEM)
    hbm = pl.BlockSpec(memory_space=pl.ANY)

    def pair(*shape):
        return [pltpu.SemaphoreType.DMA(shape), pltpu.SemaphoreType.DMA(shape)]

    return pl.pallas_call(
        functools.partial(fused_kernel, axes),
        out_shape=pltpu.VMEM((1, width, owners * slots), bf16),
        in_specs=[hbm] * 14,
        out_specs=vmem,
        scratch_shapes=[
            pltpu.VMEM(features.shape, bf16),
            pltpu.VMEM(scan_order.shape, jnp.int32),
            pltpu.SMEM(kernel_map.shape, jnp.int32),
            pltpu.SMEM(halo_send.shape, jnp.int32),
            pltpu.SMEM((1, blocks), jnp.int32),
            *[pltpu.VMEM((1, width), f32)] * 6,
            pltpu.SemaphoreType.DMA((11,)),
            pltpu.VMEM((even_taps * width, channels), bf16),
            pltpu.VMEM((even_taps * width, channels), bf16),
            pltpu.VMEM(wd.shape, bf16),
            pltpu.VMEM((owners, BLK, channels), bf16),
            pltpu.VMEM((blocks, BLK, channels), bf16),
            pltpu.VMEM((2, hcap, BLK, channels), bf16),
            pltpu.VMEM((2, hcap, BLK, channels), bf16),
            pltpu.VMEM((blocks, BLK, width), bf16),
            pltpu.VMEM((n_chan - 1, blocks, BLK, width), bf16),
            pltpu.VMEM((2, hcap, BLK, width), bf16),
            pltpu.VMEM((2, n_chan, hcap, BLK, width), bf16),
            pltpu.VMEM((even_taps, blocks + 2 * hcap + 1, BLK, width), f32),
            pltpu.VMEM((wd.shape[0], blocks, cells, width), f32),
            pltpu.VMEM((owners * slots, blocks * cells), bf16),
            pltpu.VMEM((n_chan, owners, slots, width), bf16),
            pltpu.VMEM((n_chan, owners, slots, width), bf16),
            pltpu.SemaphoreType.DMA((2 + n_chan,)),
            *pair(owners - 1),
            *pair(n_chan - 1, owners),
            *pair(2),
            *pair(n_chan - 1, groups),
            *pair(2, n_chan),
            *pair(n_chan, owners),
        ],
        compiler_params=pltpu.CompilerParams(
            collective_id=0, has_side_effects=True, vmem_limit_bytes=66977792
        ),
        name="encoder_level",
    )(
        features,
        scan_order,
        kernel_map,
        halo_send,
        down_route.reshape(1, blocks),
        w1.reshape(taps * width, channels),
        w2.reshape(taps * width, channels),
        wd,
        *[scale.reshape(1, width) for scale in scales],
    )


def fits(axes, features, kernel_map, width):
    n_brick, n_chan, n_sub = axes
    owners = n_brick * n_sub
    whole = width % LANES == 0 and n_chan > 1 and kernel_map.shape[0] % 4 == 0
    whole = whole and owners & (owners - 1) == 0 and n_sub & (n_sub - 1) == 0
    return whole and features.shape[0] == owners * BLK and kernel_map.shape[0] == owners * n_chan


def from_behind(block, axis, distance):
    devices = range(lax.axis_size(axis))
    route = [(i - distance, i) for i in devices if i - distance in devices]
    return lax.ppermute(block, axis, route)


def neighbours(blocks, step_by):
    return from_behind(blocks, ("brick", "sub"), step_by)


def picked(index, source):
    chosen = jnp.arange(source.shape[0], dtype=jnp.int32)[None, :] == index[:, None]
    flat = source.reshape(source.shape[0], -1)
    rows = jnp.dot(chosen.astype(source.dtype), flat, preferred_element_type=jnp.float32)
    return rows.astype(source.dtype).reshape(index.shape[0], *source.shape[1:])


def convolve(extended, weight, kernel_map):
    block_count = kernel_map.shape[0]

    def one_tap(running, inputs):
        tap_weight, index = inputs
        return running + jnp.einsum(
            "brc,dc->brd",
            picked(index, extended),
            tap_weight,
            preferred_element_type=jnp.float32,
        ), None

    initial = jnp.zeros((block_count, BLK, weight.shape[1]), jnp.float32)
    running, _ = lax.scan(one_tap, initial, (weight, kernel_map.T))
    return running


def body(
    features,
    scan_order,
    kernel_map,
    halo_send,
    down_route,
    conv1_weight,
    conv2_weight,
    down_weight,
    gain_first,
    bias_first,
    gain_second,
    bias_second,
    gain_down,
    bias_down,
):
    axes = tuple(lax.axis_size(name) for name in ("brick", "chan", "sub"))
    if fits(axes, features, kernel_map, conv1_weight.shape[1]):
        return fused(
            axes,
            features,
            scan_order,
            kernel_map,
            halo_send,
            down_route,
            conv1_weight,
            conv2_weight,
            down_weight,
            gain_first,
            bias_first,
            gain_second,
            bias_second,
            gain_down,
            bias_down,
        )
    owners = lax.axis_size(("brick", "sub"))
    per_owner = features.shape[0] // owners
    channels = features.shape[1]
    width_out = conv1_weight.shape[1]
    block_count = kernel_map.shape[0]
    channel_start = lax.axis_index("chan") * width_out
    ordered = picked(scan_order[0], features).reshape(owners, per_owner, channels)
    regrouped = lax.all_to_all(ordered, ("brick", "sub"), split_axis=0, concat_axis=0, tiled=True)
    owner_rows = lax.all_gather(regrouped, "chan", axis=1, tiled=True)
    row_blocks = owner_rows.reshape(block_count, BLK, channels)

    def extend(own):
        from_lower = neighbours(picked(halo_send[0], own), 1)
        from_upper = neighbours(picked(halo_send[1], own), -1)
        empty = jnp.zeros((1, BLK, channels), jnp.bfloat16)
        return jnp.concatenate([own, from_lower, from_upper, empty], axis=0)

    conv_first = convolve(extend(row_blocks), conv1_weight, kernel_map)
    hidden = jax.nn.relu(conv_first * gain_first + bias_first).astype(jnp.bfloat16)
    all_channels = lax.all_gather(hidden, "chan", axis=2, tiled=True)
    second = convolve(extend(all_channels), conv2_weight, kernel_map)
    residual = lax.dynamic_slice_in_dim(row_blocks, channel_start, width_out, 2)
    refined = jax.nn.relu(second * gain_second + bias_second + residual.astype(jnp.float32))
    children = refined.astype(jnp.bfloat16).reshape(block_count, 8, 8, width_out)
    partial_value = jnp.einsum(
        "oic,noqi->cnq", down_weight, children, preferred_element_type=jnp.float32
    )
    coarse = lax.psum_scatter(
        partial_value.reshape(width_out * lax.axis_size("chan"), block_count * 8).astype(
            jnp.bfloat16
        ),
        "chan",
        scatter_dimension=0,
        tiled=True,
    ).astype(jnp.float32)
    tile_values = jax.nn.relu(coarse * gain_down[:, None] + bias_down[:, None]).astype(jnp.bfloat16)
    tile_values = tile_values.reshape(width_out, block_count, 8)
    capacity = max(2, 2 * block_count // owners)
    destination = down_route[:, 0]
    number = jnp.arange(block_count, dtype=jnp.int32)
    alike = (destination[:, None] == destination[None, :]) & (number[:, None] > number[None, :])
    position = destination * capacity + jnp.sum(alike.astype(jnp.int32), axis=1)
    selector = (
        position[None, :] == jnp.arange(owners * capacity, dtype=jnp.int32)[:, None]
    ).astype(jnp.bfloat16)
    outgoing = jnp.einsum(
        "pn,cnq->cpq", selector, tile_values, preferred_element_type=jnp.float32
    ).astype(jnp.bfloat16)
    outgoing = outgoing.reshape(width_out, owners, capacity * 8)
    arrived = lax.all_to_all(outgoing, ("brick", "sub"), split_axis=1, concat_axis=2, tiled=True)
    return arrived.reshape(1, width_out, owners * capacity * 8)


def solution(mesh):
    placed = (
        P(("groups", "brick", "chan", "sub"), None),
        P(("groups", "brick", "chan", "sub"), None),
        P(("groups", "brick", "sub"), None),
        P(("groups", "brick", "sub"), None),
        P(("groups", "brick", "sub"), None),
        P(None, "chan", None),
        P(None, "chan", None),
        P(None, "chan", None),
        P("chan"),
        P("chan"),
        P("chan"),
        P("chan"),
        P("chan"),
        P("chan"),
    )
    return jax.shard_map(
        body,
        mesh=mesh,
        in_specs=placed,
        out_specs=P(("groups", "brick", "sub"), "chan", None),
        check_vma=False,
    )
```

```python
import functools

import jax
import jax.numpy as jnp
from jax import lax
from jax.experimental import pallas as pl
from jax.experimental.pallas import tpu as pltpu
from jax.sharding import PartitionSpec as P

BLK = 64
LANES = 128
MESH = pl.DeviceIdType.MESH


def products(lhs, weight, prod, place):
    width = prod.shape[3]
    shape = (lhs.shape[0] // BLK, BLK, width)

    def step(pair, carry):
        both = weight[pl.ds(pl.multiple_of(pair * 2 * width, 2 * width), 2 * width), :]
        result = lax.dot_general(
            lhs, both, (((1,), (1,)), ((), ())), preferred_element_type=jnp.float32
        )
        prod[2 * pair, place] = result[:, :width].reshape(shape)
        prod[2 * pair + 1, place] = result[:, width:].reshape(shape)
        return carry

    lax.fori_loop(0, prod.shape[0] // 2, step, 0, unroll=True)


def gathered_sum(prod, kernel_map, n):
    total = None
    for k in range(kernel_map.shape[1]):
        term = prod[k, kernel_map[n, k]]
        total = term if total is None else total + term
    return total


def flip(x, bits):
    result = x
    weight = 1
    while weight <= bits:
        if bits & weight:
            result = result + weight - 2 * weight * lax.rem(lax.div(x, weight), 2)
        weight *= 2
    return result


def fused_kernel(
    axes,
    features_hbm,
    scan_order_hbm,
    kernel_map_hbm,
    halo_send_hbm,
    down_route_hbm,
    conv1_hbm,
    conv2_hbm,
    down_hbm,
    gain_first_hbm,
    bias_first_hbm,
    gain_second_hbm,
    bias_second_hbm,
    gain_down_hbm,
    bias_down_hbm,
    out,
    features,
    scan_order,
    kernel_map,
    halo_send,
    down_route,
    gain_first,
    bias_first,
    gain_second,
    bias_second,
    gain_down,
    bias_down,
    stage_sem,
    conv1_w,
    conv2_w,
    down_w,
    ordered,
    ext,
    halo_out,
    halo_in,
    hid_own,
    hid_in,
    hid_halo_out,
    hid_halo_in,
    prod,
    kids_ref,
    selector,
    tile_out,
    tile_in,
    w_sem,
    a2a_s,
    a2a_r,
    fwd_s,
    fwd_r,
    halo_s,
    halo_r,
    hid_s,
    hid_r,
    hh_s,
    hh_r,
    tile_s,
    tile_r,
):
    staged = [
        pltpu.make_async_copy(source, place, stage_sem.at[i])
        for i, (source, place) in enumerate(
            [
                (features_hbm, features),
                (scan_order_hbm, scan_order),
                (kernel_map_hbm, kernel_map),
                (halo_send_hbm, halo_send),
                (down_route_hbm, down_route),
                (gain_first_hbm, gain_first),
                (bias_first_hbm, bias_first),
                (gain_second_hbm, gain_second),
                (bias_second_hbm, bias_second),
                (gain_down_hbm, gain_down),
                (bias_down_hbm, bias_down),
            ]
        )
    ]
    for load in staged:
        load.start()
    n_brick, n_chan, n_sub = axes
    owners = n_brick * n_sub
    blocks = kernel_map.shape[0]
    channels = features.shape[1]
    width = out.shape[1]
    hcap = halo_send.shape[1]
    group_count = hid_s.shape[1]
    group = blocks // group_count
    me_group = lax.axis_index("groups")
    chan = lax.axis_index("chan")
    me = lax.axis_index("brick") * n_sub + lax.axis_index("sub")
    own_cols = pl.ds(pl.multiple_of(chan * width, LANES), width)

    def device(owner, c):
        return (me_group, lax.div(owner, n_sub), c, lax.rem(owner, n_sub))

    def owner_at(shift):
        return lax.rem(me + shift + owners, owners)

    def chan_at(shift):
        return lax.rem(chan + shift + n_chan, n_chan)

    def remote(src, dst, send, recv, target):
        return pltpu.make_async_remote_copy(
            src_ref=src,
            dst_ref=dst,
            send_sem=send,
            recv_sem=recv,
            device_id=target,
            device_id_type=MESH,
        )

    taps = kernel_map.shape[1]
    loads = [
        pltpu.make_async_copy(conv1_hbm, conv1_w.at[pl.ds(0, taps * width)], w_sem.at[0]),
        pltpu.make_async_copy(down_hbm, down_w, w_sem.at[1]),
    ]

    def cols_from(j):
        return pl.ds(pl.multiple_of(chan_at(-j) * width, LANES), width)

    for j in range(n_chan):
        target = conv2_w.at[pl.ds(0, taps * width), pl.ds(j * width, width)]
        loads.append(
            pltpu.make_async_copy(conv2_hbm.at[:, cols_from(j)], target, w_sem.at[2 + j])
        )
    barrier = pltpu.get_barrier_semaphore()
    partners = [device(flip(me, i), chan) for i in reversed(range(1, owners))]
    partners += [device(me, chan_at(j)) for j in range(1, n_chan)]
    for partner in partners:
        pl.semaphore_signal(barrier, inc=1, device_id=partner, device_id_type=MESH)
    for load in loads:
        load.start()

    for load in staged[:2]:
        load.wait()
    count = features.shape[0]
    source_row = lax.broadcasted_iota(jnp.int32, (count, count), 0)
    chosen = jnp.where(source_row == scan_order[...], 1.0, 0.0).astype(jnp.bfloat16)
    rows = lax.dot_general(
        chosen, features[...], (((0,), (0,)), ((), ())), preferred_element_type=jnp.float32
    ).astype(jnp.bfloat16)
    ordered[...] = rows.reshape(owners, BLK, channels)

    pl.semaphore_wait(barrier, len(partners))

    pending = []
    a2a = []
    for i in range(1, owners):
        target = flip(me, i)
        a2a.append(
            remote(
                ordered.at[target],
                ext.at[me * n_chan + chan],
                a2a_s.at[i - 1],
                a2a_r.at[i - 1],
                device(target, chan),
            )
        )
    for copy in a2a:
        copy.start()
    pending += a2a

    def forward(i, src):
        block = flip(me, i) * n_chan + chan
        for j in range(1, n_chan):
            copy = remote(
                src,
                ext.at[block],
                fwd_s.at[j - 1, i],
                fwd_r.at[j - 1, i],
                device(me, chan_at(j)),
            )
            copy.start()
            forwards[i].append(copy)

    forwards = [[] for _ in range(owners)]
    brick_blocks = n_sub * n_chan

    def pass_on(m):
        for i in range(m * n_sub, (m + 1) * n_sub):
            if i == 0:
                forward(0, ordered.at[me])
                ext[me * n_chan + chan] = ordered[me]
            else:
                a2a[i - 1].wait_recv()
                forward(i, ext.at[flip(me, i) * n_chan + chan])

    def collect(m):
        for i in range(m * n_sub, (m + 1) * n_sub):
            for copy in forwards[i]:
                copy.wait_recv()

    def multiply(m):
        place = pl.ds(flip(lax.axis_index("brick"), m) * brick_blocks, brick_blocks)
        products(ext[place].reshape(brick_blocks * BLK, channels), conv1_w, prod, place)

    pass_on(0)
    spare = conv1_w.shape[0] - taps * width
    if spare:
        conv1_w[pl.ds(taps * width, spare), :] = jnp.zeros((spare, channels), jnp.bfloat16)
        conv2_w[pl.ds(taps * width, spare), :] = jnp.zeros((spare, channels), jnp.bfloat16)
    for k in range(taps):
        prod[k, blocks + 2 * hcap] = jnp.zeros((BLK, width), jnp.float32)

    for load in staged[2:]:
        load.wait()
    slots = tile_out.shape[2]
    kids = down_w.shape[0]
    cells = BLK // kids
    capacity = slots // cells
    column = lax.broadcasted_iota(jnp.int32, (1, blocks * cells), 1)
    target_row = lax.rem(column, cells)
    names = [down_route[0, n] for n in range(blocks)]
    for n in range(blocks):
        earlier = jnp.int32(0)
        for before in range(n):
            earlier = earlier + jnp.where(names[before] == names[n], 1, 0)
        position = (names[n] * capacity + earlier) * cells
        target_row = target_row + jnp.where(lax.div(column, cells) == n, position, 0)
    slot_row = lax.broadcasted_iota(jnp.int32, (owners * slots, blocks * cells), 0)
    selector[...] = jnp.where(slot_row == target_row, 1.0, 0.0).astype(jnp.bfloat16)
    loads[0].wait()
    for m in range(1, n_brick):
        pass_on(m)
    for m in range(n_brick - 1):
        collect(m)
        multiply(m)
    collect(n_brick - 1)
    pending += [copy for copies in forwards for copy in copies]

    has_next, has_last = me < owners - 1, me > 0

    def halo_copies(direction):
        return remote(
            halo_out.at[direction],
            halo_in.at[direction],
            halo_s.at[direction],
            halo_r.at[direction],
            device(owner_at(1 if direction == 0 else -1), chan),
        )

    for direction, sends in ((1, has_last), (0, has_next)):
        for j in range(hcap):
            halo_out[direction, j] = ext[halo_send[direction, j]]
        pl.when(sends)(lambda direction=direction: halo_copies(direction).start())
    multiply(n_brick - 1)
    for direction, receives in ((0, has_last), (1, has_next)):

        @pl.when(receives)
        def _():
            halo_copies(direction).wait_recv()

        @pl.when(jnp.logical_not(receives))
        def _():
            halo_in[direction] = jnp.zeros((hcap, BLK, channels), jnp.bfloat16)

    rim = pl.ds(blocks, 2 * hcap)
    products(halo_in[...].reshape(2 * hcap * BLK, channels), conv1_w, prod, rim)

    def first_hidden(n):
        scaled = gathered_sum(prod, kernel_map, n) * gain_first[...] + bias_first[...]
        return jnp.maximum(scaled, 0.0).astype(jnp.bfloat16)

    def hid_halo_copies(direction):
        return [
            remote(
                hid_halo_out.at[direction],
                hid_halo_in.at[direction, j],
                hh_s.at[direction, j],
                hh_r.at[direction, j],
                device(owner_at(1 if direction == 0 else -1), chan_at(j)),
            )
            for j in range(n_chan)
        ]

    def send_hidden_rim(direction, sends):
        for j in range(hcap):
            hid_halo_out[direction, j] = first_hidden(halo_send[direction, j])

        @pl.when(sends)
        def _():
            for copy in hid_halo_copies(direction):
                copy.start()

    send_hidden_rim(1, has_last)
    hid_copies = []
    for g in range(group_count):

        def first_block(n, carry):
            hid_own[n] = first_hidden(n)
            return carry

        lax.fori_loop(g * group, (g + 1) * group, first_block, 0, unroll=2)
        place = pl.ds(g * group, group)
        for j in range(1, n_chan):
            copy = remote(
                hid_own.at[place],
                hid_in.at[j - 1, place],
                hid_s.at[j - 1, g],
                hid_r.at[j - 1, g],
                device(me, chan_at(j)),
            )
            copy.start()
            hid_copies.append(copy)
        if g == 0:
            send_hidden_rim(0, has_next)
    pending += hid_copies

    for load in loads[2:]:
        load.wait()
    def second_products(g):
        place = pl.ds(g * group, group)
        halves = [hid_own[place]]
        for j in range(1, n_chan):
            hid_copies[g * (n_chan - 1) + j - 1].wait_recv()
            halves.append(hid_in[j - 1, place])
        lhs = jnp.concatenate([half.reshape(group * BLK, width) for half in halves], axis=1)
        products(lhs, conv2_w, prod, place)

    for g in range(group_count - 1):
        second_products(g)
    for direction, receives in ((0, has_last), (1, has_next)):

        @pl.when(receives)
        def _():
            for copy in hid_halo_copies(direction):
                copy.wait_recv()

        @pl.when(jnp.logical_not(receives))
        def _():
            hid_halo_in[direction] = jnp.zeros(hid_halo_in.shape[1:], jnp.bfloat16)

    halves = [hid_halo_in[:, j].reshape(2 * hcap * BLK, width) for j in range(n_chan)]
    products(jnp.concatenate(halves, axis=1), conv2_w, prod, rim)
    second_products(group_count - 1)
    loads[1].wait()

    def second_block(n, carry):
        second = gathered_sum(prod, kernel_map, n)
        residual = ext[n, :, own_cols].astype(jnp.float32)
        refined = jnp.maximum(second * gain_second[...] + bias_second[...] + residual, 0.0)
        refined = refined.reshape(kids, cells, width)
        for o in range(kids):
            kids_ref[o, n] = refined[o]
        return carry

    lax.fori_loop(0, blocks, second_block, 0, unroll=4)
    partial = None
    for o in range(0, kids, 2):
        child = jnp.concatenate(
            [kids_ref[o + h].reshape(blocks * cells, width) for h in range(2)], axis=1
        ).astype(jnp.bfloat16)
        weight = down_w[o : o + 2].reshape(2 * width, channels)
        product = jnp.dot(child, weight, preferred_element_type=jnp.float32)
        partial = product if partial is None else partial + product
    mine = [chan == c for c in range(n_chan)]
    scale = jnp.concatenate([jnp.where(own, gain_down[...], 1.0) for own in mine], axis=1)
    shift = jnp.concatenate([jnp.where(own, bias_down[...], 0.0) for own in mine], axis=1)
    sides = (partial * scale + shift).astype(jnp.bfloat16)
    def pack_tiles(first, last):
        chosen = selector[first * slots : last * slots, :]
        outgoing = jnp.dot(chosen, sides, preferred_element_type=jnp.float32)
        for c in range(n_chan):
            half = outgoing[:, c * width : (c + 1) * width].astype(jnp.bfloat16)
            tile_out[c, first:last] = half.reshape(last - first, slots, width)

    def send_tile(c, target):
        side = lax.rem(c - chan + n_chan, n_chan)
        copy = remote(
            tile_out.at[c, target],
            tile_in.at[side, me],
            tile_s.at[side, target],
            tile_r.at[side, me],
            device(target, c),
        )
        pl.when(jnp.logical_or(me != target, chan != c))(copy.start)

    def tiles(act):
        for other in range(owners):
            for side in range(n_chan):
                copy = remote(
                    tile_out.at[side, other],
                    tile_in.at[side, other],
                    tile_s.at[side, other],
                    tile_r.at[side, other],
                    device(other, chan_at(side)),
                )
                if side:
                    act(copy)
                else:
                    pl.when(me != other)(functools.partial(act, copy))

    pack_tiles(0, n_sub)
    for c in range(n_chan):
        for target in range(n_sub):
            send_tile(c, target)
    pack_tiles(n_sub, owners)
    for target in reversed(range(n_sub, owners)):
        for c in range(n_chan):
            send_tile(c, target)
    tile_in[0, me] = tile_out[chan, me]
    for copy in pending:
        copy.wait_send()
    for direction, sends in ((0, has_next), (1, has_last)):

        @pl.when(sends)
        def _():
            halo_copies(direction).wait_send()
            for copy in hid_halo_copies(direction):
                copy.wait_send()

    tiles(lambda copy: copy.wait_recv())
    arrived = tile_in[0].reshape(owners * slots, width).astype(jnp.float32)
    for j in range(1, n_chan):
        other = tile_in[j].reshape(owners * slots, width).astype(jnp.float32)
        arrived = arrived + other * gain_down[...]
    out[0] = jnp.maximum(arrived, 0.0).T.astype(jnp.bfloat16)
    tiles(lambda copy: copy.wait_send())


def fused(axes, features, scan_order, kernel_map, halo_send, down_route, w1, w2, wd, *scales):
    n_brick, n_chan, n_sub = axes
    owners = n_brick * n_sub
    blocks = kernel_map.shape[0]
    channels = features.shape[1]
    width = w1.shape[1]
    hcap = halo_send.shape[1]
    taps = kernel_map.shape[1]
    even_taps = taps + taps % 2
    cells = BLK // wd.shape[0]
    slots = max(2, 2 * blocks // owners) * cells
    groups = 4
    bf16, f32 = jnp.bfloat16, jnp.float32
    vmem = pl.BlockSpec(memory_space=pltpu.VMEM)
    hbm = pl.BlockSpec(memory_space=pl.ANY)

    def pair(*shape):
        return [pltpu.SemaphoreType.DMA(shape), pltpu.SemaphoreType.DMA(shape)]

    return pl.pallas_call(
        functools.partial(fused_kernel, axes),
        out_shape=pltpu.VMEM((1, width, owners * slots), bf16),
        in_specs=[hbm] * 14,
        out_specs=vmem,
        scratch_shapes=[
            pltpu.VMEM(features.shape, bf16),
            pltpu.VMEM(scan_order.shape, jnp.int32),
            pltpu.SMEM(kernel_map.shape, jnp.int32),
            pltpu.SMEM(halo_send.shape, jnp.int32),
            pltpu.SMEM((1, blocks), jnp.int32),
            *[pltpu.VMEM((1, width), f32)] * 6,
            pltpu.SemaphoreType.DMA((11,)),
            pltpu.VMEM((even_taps * width, channels), bf16),
            pltpu.VMEM((even_taps * width, channels), bf16),
            pltpu.VMEM(wd.shape, bf16),
            pltpu.VMEM((owners, BLK, channels), bf16),
            pltpu.VMEM((blocks, BLK, channels), bf16),
            pltpu.VMEM((2, hcap, BLK, channels), bf16),
            pltpu.VMEM((2, hcap, BLK, channels), bf16),
            pltpu.VMEM((blocks, BLK, width), bf16),
            pltpu.VMEM((n_chan - 1, blocks, BLK, width), bf16),
            pltpu.VMEM((2, hcap, BLK, width), bf16),
            pltpu.VMEM((2, n_chan, hcap, BLK, width), bf16),
            pltpu.VMEM((even_taps, blocks + 2 * hcap + 1, BLK, width), f32),
            pltpu.VMEM((wd.shape[0], blocks, cells, width), f32),
            pltpu.VMEM((owners * slots, blocks * cells), bf16),
            pltpu.VMEM((n_chan, owners, slots, width), bf16),
            pltpu.VMEM((n_chan, owners, slots, width), bf16),
            pltpu.SemaphoreType.DMA((2 + n_chan,)),
            *pair(owners - 1),
            *pair(n_chan - 1, owners),
            *pair(2),
            *pair(n_chan - 1, groups),
            *pair(2, n_chan),
            *pair(n_chan, owners),
        ],
        compiler_params=pltpu.CompilerParams(
            collective_id=0, has_side_effects=True, vmem_limit_bytes=66977792
        ),
        name="encoder_level",
    )(
        features,
        scan_order,
        kernel_map,
        halo_send,
        down_route.reshape(1, blocks),
        w1.reshape(taps * width, channels),
        w2.reshape(taps * width, channels),
        wd,
        *[scale.reshape(1, width) for scale in scales],
    )


def fits(axes, features, kernel_map, width):
    n_brick, n_chan, n_sub = axes
    owners = n_brick * n_sub
    whole = width % LANES == 0 and n_chan > 1 and kernel_map.shape[0] % 4 == 0
    whole = whole and owners & (owners - 1) == 0 and n_sub & (n_sub - 1) == 0
    return whole and features.shape[0] == owners * BLK and kernel_map.shape[0] == owners * n_chan


def from_behind(block, axis, distance):
    devices = range(lax.axis_size(axis))
    route = [(i - distance, i) for i in devices if i - distance in devices]
    return lax.ppermute(block, axis, route)


def neighbours(blocks, step_by):
    return from_behind(blocks, ("brick", "sub"), step_by)


def picked(index, source):
    chosen = jnp.arange(source.shape[0], dtype=jnp.int32)[None, :] == index[:, None]
    flat = source.reshape(source.shape[0], -1)
    rows = jnp.dot(chosen.astype(source.dtype), flat, preferred_element_type=jnp.float32)
    return rows.astype(source.dtype).reshape(index.shape[0], *source.shape[1:])


def convolve(extended, weight, kernel_map):
    block_count = kernel_map.shape[0]

    def one_tap(running, inputs):
        tap_weight, index = inputs
        return running + jnp.einsum(
            "brc,dc->brd",
            picked(index, extended),
            tap_weight,
            preferred_element_type=jnp.float32,
        ), None

    initial = jnp.zeros((block_count, BLK, weight.shape[1]), jnp.float32)
    running, _ = lax.scan(one_tap, initial, (weight, kernel_map.T))
    return running


def body(
    features,
    scan_order,
    kernel_map,
    halo_send,
    down_route,
    conv1_weight,
    conv2_weight,
    down_weight,
    gain_first,
    bias_first,
    gain_second,
    bias_second,
    gain_down,
    bias_down,
):
    axes = tuple(lax.axis_size(name) for name in ("brick", "chan", "sub"))
    if fits(axes, features, kernel_map, conv1_weight.shape[1]):
        return fused(
            axes,
            features,
            scan_order,
            kernel_map,
            halo_send,
            down_route,
            conv1_weight,
            conv2_weight,
            down_weight,
            gain_first,
            bias_first,
            gain_second,
            bias_second,
            gain_down,
            bias_down,
        )
    owners = lax.axis_size(("brick", "sub"))
    per_owner = features.shape[0] // owners
    channels = features.shape[1]
    width_out = conv1_weight.shape[1]
    block_count = kernel_map.shape[0]
    channel_start = lax.axis_index("chan") * width_out
    ordered = picked(scan_order[0], features).reshape(owners, per_owner, channels)
    regrouped = lax.all_to_all(ordered, ("brick", "sub"), split_axis=0, concat_axis=0, tiled=True)
    owner_rows = lax.all_gather(regrouped, "chan", axis=1, tiled=True)
    row_blocks = owner_rows.reshape(block_count, BLK, channels)

    def extend(own):
        from_lower = neighbours(picked(halo_send[0], own), 1)
        from_upper = neighbours(picked(halo_send[1], own), -1)
        empty = jnp.zeros((1, BLK, channels), jnp.bfloat16)
        return jnp.concatenate([own, from_lower, from_upper, empty], axis=0)

    conv_first = convolve(extend(row_blocks), conv1_weight, kernel_map)
    hidden = jax.nn.relu(conv_first * gain_first + bias_first).astype(jnp.bfloat16)
    all_channels = lax.all_gather(hidden, "chan", axis=2, tiled=True)
    second = convolve(extend(all_channels), conv2_weight, kernel_map)
    residual = lax.dynamic_slice_in_dim(row_blocks, channel_start, width_out, 2)
    refined = jax.nn.relu(second * gain_second + bias_second + residual.astype(jnp.float32))
    children = refined.astype(jnp.bfloat16).reshape(block_count, 8, 8, width_out)
    partial_value = jnp.einsum(
        "oic,noqi->cnq", down_weight, children, preferred_element_type=jnp.float32
    )
    coarse = lax.psum_scatter(
        partial_value.reshape(width_out * lax.axis_size("chan"), block_count * 8).astype(
            jnp.bfloat16
        ),
        "chan",
        scatter_dimension=0,
        tiled=True,
    ).astype(jnp.float32)
    tile_values = jax.nn.relu(coarse * gain_down[:, None] + bias_down[:, None]).astype(jnp.bfloat16)
    tile_values = tile_values.reshape(width_out, block_count, 8)
    capacity = max(2, 2 * block_count // owners)
    destination = down_route[:, 0]
    number = jnp.arange(block_count, dtype=jnp.int32)
    alike = (destination[:, None] == destination[None, :]) & (number[:, None] > number[None, :])
    position = destination * capacity + jnp.sum(alike.astype(jnp.int32), axis=1)
    selector = (
        position[None, :] == jnp.arange(owners * capacity, dtype=jnp.int32)[:, None]
    ).astype(jnp.bfloat16)
    outgoing = jnp.einsum(
        "pn,cnq->cpq", selector, tile_values, preferred_element_type=jnp.float32
    ).astype(jnp.bfloat16)
    outgoing = outgoing.reshape(width_out, owners, capacity * 8)
    arrived = lax.all_to_all(outgoing, ("brick", "sub"), split_axis=1, concat_axis=2, tiled=True)
    return arrived.reshape(1, width_out, owners * capacity * 8)


def solution(mesh):
    placed = (
        P(("groups", "brick", "chan", "sub"), None),
        P(("groups", "brick", "chan", "sub"), None),
        P(("groups", "brick", "sub"), None),
        P(("groups", "brick", "sub"), None),
        P(("groups", "brick", "sub"), None),
        P(None, "chan", None),
        P(None, "chan", None),
        P(None, "chan", None),
        P("chan"),
        P("chan"),
        P("chan"),
        P("chan"),
        P("chan"),
        P("chan"),
    )
    return jax.shard_map(
        body,
        mesh=mesh,
        in_specs=placed,
        out_specs=P(("groups", "brick", "sub"), "chan", None),
        check_vma=False,
    )
```
